512 devices in a mesh: ctx: 256 (over z, y, x), tp: 2 (over core).
Axes of the slice: x: 4, y: 8, z: 8, core: 2. Of those that a mesh axis runs over, the one named last changes fastest.
Arguments:
- queries: bfloat16 [32768, 64, 128], P(('ctx', 'tp')), may hold values from -24 to 24
- rotated_key_rows: bfloat16 [32768, 8, 128], P(('ctx', 'tp')), may hold values from -24 to 24
- unscaled_value_rows: bfloat16 [32768, 8, 128], P(('ctx', 'tp')), may hold values from -6 to 6
- key_block_scales: bfloat16 [256, 8], P('ctx', 'tp'), may hold values from 0.5 to 2
- value_block_scales: bfloat16 [256, 8], P('ctx', 'tp'), may hold values from 0.5 to 2
- doc_lengths: int32 [256], replicated, may hold values from 1 to 512, 32768 in all
Outputs:
- attended: bfloat16 [32768, 64, 128], P(('ctx', 'tp'))
The draws below stay inside these ranges and needn't reach their ends.
Inputs may be any that keep to these rules, and one draw needn't show every extreme that they name: `doc_lengths`: they sum to 32768; the longest is exactly 512.
All inputs are finite; a program needn't handle non-finite values.
Results may differ from the reference program's by a relative error of at most 0.0035.
Values may be sent and summed in bfloat16 or wider, within the bound.
A program may use at most 64 MiB of HBM per device.

```python
import math
import jax
import jax.numpy as jnp
import numpy as np
from jax import lax

QUERY_HEADS = 64
KEY_VALUE_HEADS = 8
HEAD_WIDTH = 128
SCALE_BLOCK = 128
TOKENS_PER_SHARD = 128
DOCUMENT_LIMIT = 512
PACKED_TOKENS = 32768
NDOCS = 256


def draw_queries(key, part):
    own_part = jnp.clip(jax.random.normal(jax.random.fold_in(key, 11), (PACKED_TOKENS, QUERY_HEADS, HEAD_WIDTH), jnp.float32), -4.0, 4.0)
    return own_part.astype(jnp.bfloat16)


def draw_rotated_key_rows(key, part):
    own_part = jnp.clip(jax.random.normal(jax.random.fold_in(key, 12), (PACKED_TOKENS, KEY_VALUE_HEADS, HEAD_WIDTH), jnp.float32), -4.0, 4.0)
    return own_part.astype(jnp.bfloat16)


def steps_of(stream_key, dims, cuts, smallest, high):
    def one(position, shards_of):
        heights = jax.random.uniform(jax.random.fold_in(jax.random.fold_in(stream_key, 6), position), (shards_of,), jnp.float32, smallest / len(cuts), high / len(cuts))
        return jnp.repeat(jnp.exp(heights), dims[position] // shards_of).reshape((-1,) + (1,) * (len(dims) - position - 1))

    factor_of = one(*cuts[0])
    for cut in cuts[1:]:
        factor_of = factor_of * one(*cut)
    return factor_of


def profile(count, total, limit, lean):
    portions = [(1 << 20) // math.isqrt(grade ** lean) + 1 for grade in range(2, count + 1)]
    surplus, counts = total - limit - (count - 1), [1] * (count - 1)
    while surplus > 0:
        candidates = [i for i in range(count - 1) if counts[i] < limit]
        whole, left = sum([portions[i] for i in candidates]), surplus
        for i in candidates:
            more = min(limit - counts[i], max(1, left * portions[i] // whole), surplus)
            counts[i] = counts[i] + more
            surplus = surplus - more
    return np.array([limit] + counts)


def uneven(own_key, count, total, bound, lean):
    if count == 2:
        one = jax.random.randint(own_key, (), max(1, total - bound), min(bound, total - 1) + 1)
        return jnp.stack([one, total - one])
    sizes = jnp.asarray(profile(count, total, bound, lean), jnp.int32)
    twos = (count - 1) // 2
    giver, receiver = sizes[1:1 + 2 * twos:2], sizes[2:2 + 2 * twos:2]
    slack = jnp.minimum(giver - 1, bound - receiver)
    passed = jax.random.randint(jax.random.fold_in(own_key, 1), (twos,), 0, 1 << 20) % (slack + 1)
    sizes = sizes.at[1:1 + 2 * twos:2].set(giver - passed).at[2:2 + 2 * twos:2].set(receiver + passed)
    return sizes[jax.random.permutation(jax.random.fold_in(own_key, 2), count)]


def noise(key, shape, deviation, limit, cuts=(), held_as=jnp.bfloat16):
    result = deviation * jax.random.normal(key, shape, jnp.float32)
    if cuts:
        result = result * steps_of(key, shape, cuts, -0.22, 0.18)
    return jnp.clip(result, -limit, limit).astype(held_as)


def setup_inputs(seed: int = 0) -> dict:
    seeds = jax.random.split(jax.random.key(seed), 7)
    return {
        "queries": draw_queries(jax.random.fold_in(seeds[6], 71), 0),
        "rotated_key_rows": draw_rotated_key_rows(jax.random.fold_in(seeds[6], 71), 0),
        "unscaled_value_rows": noise(seeds[2], (PACKED_TOKENS, KEY_VALUE_HEADS, HEAD_WIDTH), 1.0, 6.0, ((0, 512),)),
        "key_block_scales": jnp.clip(jnp.exp(math.log(2.0) - 1.3862944 * jax.random.uniform(seeds[3], (PACKED_TOKENS // SCALE_BLOCK, KEY_VALUE_HEADS), jnp.float32) ** steps_of(seeds[3], (PACKED_TOKENS // SCALE_BLOCK, KEY_VALUE_HEADS), ((0, 256), (1, 2)), -0.2, 0.2)), 0.5, 2.0).astype(jnp.bfloat16),
        "value_block_scales": jnp.clip(jnp.exp(math.log(2.0) - 1.3862944 * jax.random.uniform(seeds[4], (PACKED_TOKENS // SCALE_BLOCK, KEY_VALUE_HEADS), jnp.float32) ** steps_of(seeds[4], (PACKED_TOKENS // SCALE_BLOCK, KEY_VALUE_HEADS), ((0, 256), (1, 2)), -0.2, 0.2)), 0.5, 2.0).astype(jnp.bfloat16),
        "doc_lengths": uneven(seeds[5], NDOCS, PACKED_TOKENS, DOCUMENT_LIMIT, 2).astype(jnp.int32),
    }


def document_of(positions, ends):
    return lax.optimization_barrier(jnp.sum((positions[:, None] >= ends[None, :]).astype(jnp.int32), axis=1)).astype(jnp.int32)

def reference(queries, rotated_key_rows, unscaled_value_rows, key_block_scales, value_block_scales, doc_lengths):
    query_group = QUERY_HEADS // KEY_VALUE_HEADS
    token_span = DOCUMENT_LIMIT + TOKENS_PER_SHARD
    ends = jnp.cumsum(doc_lengths).astype(jnp.int32)
    key_padding = jnp.concatenate([jnp.zeros((DOCUMENT_LIMIT, KEY_VALUE_HEADS, HEAD_WIDTH), rotated_key_rows.dtype), rotated_key_rows], axis=0)
    value_padding = jnp.concatenate([jnp.zeros((DOCUMENT_LIMIT, KEY_VALUE_HEADS, HEAD_WIDTH), unscaled_value_rows.dtype), unscaled_value_rows], axis=0)
    key_scale = jnp.repeat(key_block_scales, SCALE_BLOCK, axis=0)
    value_scale = jnp.repeat(value_block_scales, SCALE_BLOCK, axis=0)
    key_scale_padding = jnp.concatenate([jnp.ones((DOCUMENT_LIMIT, KEY_VALUE_HEADS), key_scale.dtype), key_scale], axis=0)
    value_scale_padding = jnp.concatenate([jnp.ones((DOCUMENT_LIMIT, KEY_VALUE_HEADS), value_scale.dtype), value_scale], axis=0)
    pad_pos = jnp.arange(PACKED_TOKENS + DOCUMENT_LIMIT, dtype=jnp.int32) - DOCUMENT_LIMIT
    pad_doc = document_of(pad_pos, ends)

    def one_block(index):
        start_offset = (index * TOKENS_PER_SHARD).astype(jnp.int32)
        query_rows = lax.dynamic_slice_in_dim(queries, start_offset, TOKENS_PER_SHARD, 0).astype(jnp.float32)
        query_rows = query_rows.reshape(TOKENS_PER_SHARD, KEY_VALUE_HEADS, query_group, HEAD_WIDTH)
        key_vectors = lax.dynamic_slice_in_dim(key_padding, start_offset, token_span, 0).astype(jnp.float32)
        value_vectors = lax.dynamic_slice_in_dim(value_padding, start_offset, token_span, 0).astype(jnp.float32)
        key_scale_local = lax.dynamic_slice_in_dim(key_scale_padding, start_offset, token_span, 0).astype(jnp.float32)
        vscl = lax.dynamic_slice_in_dim(value_scale_padding, start_offset, token_span, 0).astype(jnp.float32)
        q_pos = start_offset + jnp.arange(TOKENS_PER_SHARD, dtype=jnp.int32)
        q_doc = document_of(q_pos, ends)
        k_pos = lax.dynamic_slice_in_dim(pad_pos, start_offset, token_span, 0)
        k_doc = lax.dynamic_slice_in_dim(pad_doc, start_offset, token_span, 0)
        allowed = (k_doc[None, :] == q_doc[:, None]) & (k_pos[None, :] <= q_pos[:, None]) & (k_pos[None, :] >= 0)
        mask_four = allowed[:, None, None, :]
        scores = jnp.einsum('qkgd,jkd->qkgj', query_rows, key_vectors) / math.sqrt(HEAD_WIDTH) * key_scale_local.T[None, :, None, :]
        scores = jnp.where(mask_four, scores, -1e+30)
        top = lax.optimization_barrier(jnp.max(scores, axis=3, keepdims=True))
        expo = jnp.where(mask_four, jnp.exp(scores - top), 0.0)
        total = lax.optimization_barrier(jnp.sum(expo, axis=3))
        weights = (expo * vscl.T[None, :, None, :]).astype(jnp.bfloat16)
        weights = lax.optimization_barrier(weights).astype(jnp.float32)
        summed = jnp.einsum('qkgj,jkd->qkgd', weights, value_vectors)
        return (summed / total[..., None]).reshape(TOKENS_PER_SHARD, QUERY_HEADS, HEAD_WIDTH).astype(jnp.bfloat16)
    blocks = lax.map(one_block, jnp.arange(PACKED_TOKENS // TOKENS_PER_SHARD, dtype=jnp.int32))
    return blocks.reshape(PACKED_TOKENS, QUERY_HEADS, HEAD_WIDTH)
```

```python
import math

import jax
import jax.numpy as jnp
from jax import lax
from jax.experimental import pallas as pl
from jax.experimental.pallas import tpu as pltpu
from jax.sharding import PartitionSpec as P

CHUNKS = 4
COLUMNS = 4
MASKED = -1e30


def relays(role, slot, chunk):
    early = chunk < CHUNKS // 2
    out = []
    if slot == 4:
        if role in (2, 3) or (role == 1 and early):
            out.append(("left", 3))
        if role == 3:
            out.append(("right", 1))
    if slot == 1:
        if early and role in (0, 1, 2):
            out.append(("right", 2))
        if role == 3 and not early:
            out.append(("next_row", 5))
    if slot == 3:
        if (role == 1 and early) or (role in (2, 3) and not early):
            out.append(("left", 2))
    if slot == 5:
        if role == 0:
            out.extend([("left", 2), ("next_row", 3)])
        if role == 3:
            out.append(("right", 2))
    return out


def first_sends(role, chunk):
    out = []
    if role == 0:
        out.append(("left", 3))
    if role == 1 and chunk >= CHUNKS // 2:
        out.append(("left", 5))
    if role in (0, 1, 2):
        out.append(("right", 1))
    return out


EARLY = [3.0, 4.4, 5.8, 7.2]
EXPECTED = {
    0: {4: EARLY, 5: [None, None, 3.0, 4.4], 3: [6.0, 7.4, 8.6, 10.0], 1: [6.0, 7.4, 8.8, 10.2],
        2: [9.0, 10.4, 11.8, 13.2]},
    1: {4: EARLY, 1: EARLY, 3: [6.0, 7.4, 8.8, 10.2], 2: [9.0, 10.4, 11.8, 13.2]},
    2: {4: EARLY, 1: EARLY, 3: [6.0, 7.4, 8.8, 10.2], 2: [8.6, 10.0, 11.6, 13.0]},
    3: {4: EARLY, 1: EARLY, 3: EARLY, 5: [None, None, 8.8, 10.2], 2: [8.6, 10.0, 8.6, 10.0]},
}


def kernel(
    q_hbm, k_hbm, v_hbm, sc_hbm, len_ref, o_ref,
    kvb, qb, qs, kvf, scf, bias, top, total, acc,
    lsem, ssem, rsem, fsem,
):
    ctx, c = lax.axis_index("ctx"), lax.axis_index("tp")
    count = lax.axis_size("ctx")
    x = lax.rem(ctx, COLUMNS)
    row = ctx - x
    half_tokens, kv_heads, group, width = qb.shape[0], qb.shape[1], qb.shape[2], qb.shape[3]
    block = 2 * half_tokens
    piece = half_tokens // CHUNKS
    rows = half_tokens * group
    where = {
        "partner": (ctx, 1 - c),
        "right": (row + lax.rem(x + 1, COLUMNS), c),
        "left": (row + lax.rem(x + COLUMNS - 1, COLUMNS), c),
        "next_row": (lax.rem(ctx + COLUMNS, count), c),
    }
    last_row = (lax.rem(ctx + count - COLUMNS, count), c)

    def part(slot, half, j):
        if j == 0:
            return kvb.at[slot, half, pl.ds(0, 2 * piece + 1)]
        return kvb.at[slot, half, pl.ds(1 + 2 * piece * j, 2 * piece)]

    staged = [[] for _ in range(CHUNKS)]
    staged[0].append(pltpu.make_async_copy(sc_hbm, kvb.at[0, c, pl.ds(0, 1)], lsem.at[0]))
    for j in range(CHUNKS):
        at = 1 + 2 * piece * j
        source = pl.ds(piece * j, piece)
        staged[j].append(
            pltpu.make_async_copy(k_hbm.at[source], kvb.at[0, c, pl.ds(at, piece)], lsem.at[1 + 2 * j])
        )
        staged[j].append(
            pltpu.make_async_copy(
                v_hbm.at[source], kvb.at[0, c, pl.ds(at + piece, piece)], lsem.at[2 + 2 * j]
            )
        )
    for copies in staged:
        for copy in copies:
            copy.start()
    q_copy = pltpu.make_async_copy(q_hbm, qb, lsem.at[1 + 2 * CHUNKS])
    q_copy.start()

    barrier = pltpu.get_barrier_semaphore()
    others = list(where.values()) + [last_row]
    for other in others:
        pl.semaphore_signal(barrier, inc=1, device_id=other, device_id_type=pl.DeviceIdType.MESH)
    pl.semaphore_wait(barrier, len(others))

    counter = [0]
    open_common = []
    open_role = {r: [] for r in range(COLUMNS)}

    def remote(src, dst, send, recv, to):
        return pltpu.make_async_remote_copy(
            src_ref=src, dst_ref=dst, send_sem=ssem.at[send], recv_sem=recv,
            device_id=where[to], device_id_type=pl.DeviceIdType.MESH,
        )

    def outgoing(slot, j, to, there, number):
        recv = fsem.at[there, j] if to == "partner" else rsem.at[there, j]
        return remote(part(slot, c, j), part(there, c, j), number, recv, to)

    def send(slot, j, to, there, opened):
        sent = (slot, j, to, there, counter[0])
        counter[0] += 1
        outgoing(*sent).start()
        opened.append(sent)

    for j in range(CHUNKS):
        for copy in staged[j]:
            copy.wait()
        send(0, j, "next_row", 4, open_common)
        after_common = counter[0]
        for r in range(COLUMNS):
            counter[0] = after_common

            @pl.when(x == r)
            def _(r=r, j=j):
                for to, there in first_sends(r, j):
                    send(0, j, to, there, open_role[r])

        counter[0] = after_common + 2
        send(0, j, "partner", 0, open_common)

    order = {}
    for r in range(COLUMNS):
        events = [
            (times[j], slot, j)
            for slot, times in EXPECTED[r].items()
            for j in range(CHUNKS)
            if times[j] is not None
        ]
        order[r] = sorted(events)

    def came_in(since, until):
        first = counter[0]
        most = first
        for r in range(COLUMNS):
            counter[0] = first

            @pl.when(x == r)
            def _(r=r):
                for time, slot, j in order[r]:
                    if not since <= time < until:
                        continue
                    there = part(slot, c, j)
                    remote(there, there, 0, rsem.at[slot, j], "partner").wait_recv()
                    for to, target in relays(r, slot, j):
                        send(slot, j, to, target, open_role[r])
                    if slot != 5:
                        send(slot, j, "partner", slot, open_role[r])

            most = max(most, counter[0])
        counter[0] = most

    def other_half(slot):
        for j in range(CHUNKS):
            there = part(slot, 1 - c, j)
            remote(there, there, 0, fsem.at[slot, j], "partner").wait_recv()

    def unpack(slot):
        for half in range(2):
            scf[slot, pl.ds(kv_heads * half, kv_heads), :] = kvb[slot, half, 0].astype(jnp.float32)
            for j in range(CHUNKS):
                at = 1 + 2 * piece * j
                to = pl.ds((half_tokens * half + piece * j) * kv_heads, piece * kv_heads)
                for which in range(2):
                    tile = kvb[slot, half, pl.ds(at + which * piece, piece)].astype(jnp.float32)
                    kvf[slot, which, to, :] = tile.reshape(piece * kv_heads, width)

    ones = jnp.ones((block, width), jnp.bfloat16)
    heads_per_core = kv_heads // 2
    factor = math.log2(math.e) / math.sqrt(width)

    def attend(slots, low, high, first=False, last=False):
        @pl.loop(low, high)
        def _(h):
            q = qs[h]
            scale_row = kv_heads * (h // heads_per_core) + lax.rem(h, heads_per_core)
            scores = []
            for s in slots:
                k = kvf[s, 0, pl.ds(h, block, stride=kv_heads), :].astype(jnp.bfloat16)
                raw = lax.dot_general(
                    q, k, (((1,), (1,)), ((), ())), preferred_element_type=jnp.float32
                )
                key_scale = scf[s, pl.ds(scale_row, 1), :] * factor
                scores.append(raw * key_scale + bias[s])
            high_score = scores[0]
            for more in scores[1:]:
                high_score = jnp.maximum(high_score, more)
            new_top = jnp.broadcast_to(jnp.max(high_score, axis=1, keepdims=True), (rows, width))
            if first:
                sums = summed = None
            else:
                old = top[h]
                new_top = jnp.maximum(new_top, old)
                shrink = jnp.exp2(old - new_top)
                sums = total[h] * shrink
                summed = acc[h] * shrink
            for s, score in zip(slots, scores):
                expo = jnp.exp2(score - new_top).astype(jnp.bfloat16)
                v = kvf[s, 1, pl.ds(h, block, stride=kv_heads), :].astype(jnp.bfloat16)
                both = jnp.dot(
                    expo, jnp.concatenate([v, ones], axis=1), preferred_element_type=jnp.float32
                )
                value_scale = scf[s, pl.ds(scale_row + heads_per_core, 1), :]
                added = both[:, :width] * value_scale
                summed = added if summed is None else summed + added
                sums = both[:, width:] if sums is None else sums + both[:, width:]
            if last:
                o_ref[:, h] = (summed / sums).reshape(half_tokens, group, width).astype(o_ref.dtype)
            else:
                top[h] = new_top
                total[h] = sums
                acc[h] = summed

    lengths = jnp.broadcast_to(len_ref[...].astype(jnp.float32), (8, len_ref.shape[1]))
    docs = len_ref.shape[1]
    upto = lax.broadcasted_iota(jnp.int32, (docs, docs), 0) <= lax.broadcasted_iota(
        jnp.int32, (docs, docs), 1
    )
    ends = jnp.dot(
        lengths, upto.astype(jnp.float32), precision=lax.Precision.HIGHEST,
        preferred_element_type=jnp.float32,
    )[0:1, :]
    offset = lax.broadcasted_iota(jnp.int32, (rows, docs), 0) // group
    here = (ctx * block + c * half_tokens + offset).astype(jnp.float32)
    start = jnp.max(jnp.where(ends <= here, ends, 0.0), axis=1, keepdims=True)
    lane = lax.broadcasted_iota(jnp.int32, (rows, block), 1)
    position = (
        ctx * block + c * half_tokens + lax.broadcasted_iota(jnp.int32, (rows, block), 0) // group
    ).astype(jnp.float32)
    for s in range(5):
        key_position = (ctx * block - s * block + lane).astype(jnp.float32)
        allowed = (key_position >= start) & (key_position <= position)
        bias[s] = jnp.where(allowed, 0.0, MASKED)

    q_copy.wait()

    @pl.loop(0, kv_heads)
    def _(h):
        qs[h] = qb[:, h].astype(jnp.float32).reshape(rows, width).astype(jnp.bfloat16)

    middle = kv_heads // 2
    other_half(0)
    unpack(0)
    came_in(0.0, 3.5)
    attend([0], 0, middle, first=True)
    came_in(3.5, 5.0)
    attend([0], middle, kv_heads, first=True)
    came_in(5.0, 7.3)
    other_half(4)
    unpack(4)
    attend([4], 0, middle)
    came_in(7.3, 8.7)
    attend([4], middle, kv_heads)
    came_in(8.7, 10.3)
    other_half(1)
    other_half(3)
    unpack(1)
    unpack(3)
    attend([1, 3], 0, middle)
    came_in(10.3, 12.0)
    attend([1, 3], middle, kv_heads)
    came_in(12.0, 99.0)
    other_half(2)
    unpack(2)
    attend([2], 0, kv_heads, last=True)

    for sent in open_common:
        outgoing(*sent).wait_send()
    for r in range(COLUMNS):

        @pl.when(x == r)
        def _(r=r):
            for sent in open_role[r]:
                outgoing(*sent).wait_send()


def shards(
    queries, rotated_key_rows, unscaled_value_rows, key_block_scales, value_block_scales, doc_lengths
):
    tokens, heads, width = queries.shape
    kv_heads = rotated_key_rows.shape[1]
    group = heads // kv_heads
    rows = tokens * group
    scales = jnp.concatenate([key_block_scales, value_block_scales], axis=1)
    scales = jnp.broadcast_to(scales[:, :, None], (1, kv_heads, width))
    any_space = pl.BlockSpec(memory_space=pl.ANY)
    vmem = pl.BlockSpec(memory_space=pltpu.VMEM)
    out = pl.pallas_call(
        kernel,
        out_shape=jax.ShapeDtypeStruct((tokens, kv_heads, group, width), jnp.bfloat16),
        in_specs=[any_space] * 4 + [vmem],
        out_specs=vmem,
        scratch_shapes=[
            pltpu.VMEM((6, 2, 2 * tokens + 1, kv_heads, width), jnp.bfloat16),
            pltpu.VMEM((tokens, kv_heads, group, width), jnp.bfloat16),
            pltpu.VMEM((kv_heads, rows, width), jnp.bfloat16),
            pltpu.VMEM((5, 2, 2 * tokens * kv_heads, width), jnp.float32),
            pltpu.VMEM((5, 2 * kv_heads, width), jnp.float32),
            pltpu.VMEM((5, rows, 2 * tokens), jnp.float32),
            pltpu.VMEM((kv_heads, rows, width), jnp.float32),
            pltpu.VMEM((kv_heads, rows, width), jnp.float32),
            pltpu.VMEM((kv_heads, rows, width), jnp.float32),
            pltpu.SemaphoreType.DMA((2 + 2 * CHUNKS,)),
            pltpu.SemaphoreType.DMA((100,)),
            pltpu.SemaphoreType.DMA((6, CHUNKS)),
            pltpu.SemaphoreType.DMA((5, CHUNKS)),
        ],
        compiler_params=pltpu.CompilerParams(
            collective_id=0, has_side_effects=True, vmem_limit_bytes=60 * 1024 * 1024
        ),
    )(
        queries.reshape(tokens, kv_heads, group, width),
        rotated_key_rows,
        unscaled_value_rows,
        scales,
        doc_lengths.reshape(1, -1),
    )
    return out.reshape(tokens, heads, width)


def solution(mesh):
    return jax.shard_map(
        shards,
        mesh=mesh,
        in_specs=(
            P(("ctx", "tp"), None, None),
            P(("ctx", "tp"), None, None),
            P(("ctx", "tp"), None, None),
            P("ctx", "tp"),
            P("ctx", "tp"),
            P(),
        ),
        out_specs=P(("ctx", "tp"), None, None),
        check_vma=False,
    )
```

```python
import math

import jax
import jax.numpy as jnp
from jax import lax
from jax.experimental import pallas as pl
from jax.experimental.pallas import tpu as pltpu
from jax.sharding import PartitionSpec as P

CHUNKS = 4
COLUMNS = 4
MASKED = -1e30
HEADS_AT_ONCE = 2
PARTS = 1


def relays(role, slot, chunk):
    early = chunk < CHUNKS // 2
    out = []
    if slot == 4:
        if role in (2, 3) or (role == 1 and early):
            out.append(("left", 3))
        if role == 3:
            out.append(("right", 1))
    if slot == 1:
        if early and role in (0, 1, 2):
            out.append(("right", 2))
        if role == 3 and not early:
            out.append(("next_row", 5))
    if slot == 3:
        if (role == 1 and early) or (role in (2, 3) and not early):
            out.append(("left", 2))
    if slot == 5:
        if role == 0:
            out.extend([("left", 2), ("next_row", 3)])
        if role == 3:
            out.append(("right", 2))
    return out


def first_sends(role, chunk):
    out = []
    if role == 0:
        out.append(("left", 3))
    if role == 1 and chunk >= CHUNKS // 2:
        out.append(("left", 5))
    if role in (0, 1, 2):
        out.append(("right", 1))
    return out


EARLY = [3.0, 4.4, 5.8, 7.2]
EXPECTED = {
    0: {4: EARLY, 5: [None, None, 3.0, 4.4], 3: [6.0, 7.4, 8.6, 10.0], 1: [6.0, 7.4, 8.8, 10.2],
        2: [9.0, 10.4, 11.8, 13.2]},
    1: {4: EARLY, 1: EARLY, 3: [6.0, 7.4, 8.8, 10.2], 2: [9.0, 10.4, 11.8, 13.2]},
    2: {4: EARLY, 1: EARLY, 3: [6.0, 7.4, 8.8, 10.2], 2: [8.6, 10.0, 11.6, 13.0]},
    3: {4: EARLY, 1: EARLY, 3: EARLY, 5: [None, None, 8.8, 10.2], 2: [8.6, 10.0, 8.6, 10.0]},
}


def kernel(
    q_hbm, k_hbm, v_hbm, sc_hbm, len_ref, o_ref,
    kvb, qb, qs, kvf, scf, bias, top, total, acc,
    lsem, ssem, rsem, fsem,
):
    ctx, c = lax.axis_index("ctx"), lax.axis_index("tp")
    count = lax.axis_size("ctx")
    x = lax.rem(ctx, COLUMNS)
    row = ctx - x
    half_tokens, kv_heads, group, width = qb.shape[0], qb.shape[1], qb.shape[2], qb.shape[3]
    block = 2 * half_tokens
    piece = half_tokens // CHUNKS
    rows = half_tokens * group
    where = {
        "partner": (ctx, 1 - c),
        "right": (row + lax.rem(x + 1, COLUMNS), c),
        "left": (row + lax.rem(x + COLUMNS - 1, COLUMNS), c),
        "next_row": (lax.rem(ctx + COLUMNS, count), c),
    }
    last_row = (lax.rem(ctx + count - COLUMNS, count), c)

    def part(slot, half, j):
        if j == 0:
            return kvb.at[slot, half, pl.ds(0, 2 * piece + 1)]
        return kvb.at[slot, half, pl.ds(1 + 2 * piece * j, 2 * piece)]

    staged = [[] for _ in range(CHUNKS)]
    staged[0].append(pltpu.make_async_copy(sc_hbm, kvb.at[0, c, pl.ds(0, 1)], lsem.at[0]))
    for j in range(CHUNKS):
        at = 1 + 2 * piece * j
        source = pl.ds(piece * j, piece)
        staged[j].append(
            pltpu.make_async_copy(k_hbm.at[source], kvb.at[0, c, pl.ds(at, piece)], lsem.at[1 + 2 * j])
        )
        staged[j].append(
            pltpu.make_async_copy(
                v_hbm.at[source], kvb.at[0, c, pl.ds(at + piece, piece)], lsem.at[2 + 2 * j]
            )
        )
    for copies in staged:
        for copy in copies:
            copy.start()
    q_copy = pltpu.make_async_copy(q_hbm, qb, lsem.at[1 + 2 * CHUNKS])
    q_copy.start()

    barrier = pltpu.get_barrier_semaphore()
    others = list(where.values()) + [last_row]
    for other in others:
        pl.semaphore_signal(barrier, inc=1, device_id=other, device_id_type=pl.DeviceIdType.MESH)
    pl.semaphore_wait(barrier, len(others))

    counter = [0]
    open_common = []
    open_role = {r: [] for r in range(COLUMNS)}

    def remote(src, dst, send, recv, to):
        return pltpu.make_async_remote_copy(
            src_ref=src, dst_ref=dst, send_sem=ssem.at[send], recv_sem=recv,
            device_id=where[to], device_id_type=pl.DeviceIdType.MESH,
        )

    def outgoing(slot, j, to, there, number):
        recv = fsem.at[there, j] if to == "partner" else rsem.at[there, j]
        return remote(part(slot, c, j), part(there, c, j), number, recv, to)

    def send(slot, j, to, there, opened):
        sent = (slot, j, to, there, counter[0])
        counter[0] += 1
        outgoing(*sent).start()
        opened.append(sent)

    for j in range(CHUNKS):
        for copy in staged[j]:
            copy.wait()
        send(0, j, "next_row", 4, open_common)
        after_common = counter[0]
        for r in range(COLUMNS):
            counter[0] = after_common

            @pl.when(x == r)
            def _(r=r, j=j):
                for to, there in first_sends(r, j):
                    send(0, j, to, there, open_role[r])

        counter[0] = after_common + 2
        send(0, j, "partner", 0, open_common)

    order = {}
    for r in range(COLUMNS):
        events = [
            (times[j], slot, j)
            for slot, times in EXPECTED[r].items()
            for j in range(CHUNKS)
            if times[j] is not None
        ]
        order[r] = sorted(events)

    def came_in(since, until):
        first = counter[0]
        most = first
        for r in range(COLUMNS):
            counter[0] = first

            @pl.when(x == r)
            def _(r=r):
                for time, slot, j in order[r]:
                    if not since <= time < until:
                        continue
                    there = part(slot, c, j)
                    remote(there, there, 0, rsem.at[slot, j], "partner").wait_recv()
                    for to, target in relays(r, slot, j):
                        send(slot, j, to, target, open_role[r])
                    if slot != 5:
                        send(slot, j, "partner", slot, open_role[r])

            most = max(most, counter[0])
        counter[0] = most

    def other_half(slot):
        for j in range(CHUNKS):
            there = part(slot, 1 - c, j)
            remote(there, there, 0, fsem.at[slot, j], "partner").wait_recv()

    def unpack(slot):
        for half in range(2):
            scf[slot, pl.ds(kv_heads * half, kv_heads), :] = kvb[slot, half, 0].astype(jnp.float32)
            for j in range(CHUNKS):
                at = 1 + 2 * piece * j
                to = pl.ds((half_tokens * half + piece * j) * kv_heads, piece * kv_heads)
                for which in range(2):
                    tile = kvb[slot, half, pl.ds(at + which * piece, piece)].astype(jnp.float32)
                    kvf[slot, which, to, :] = tile.reshape(piece * kv_heads, width)

    ones = jnp.ones((block, width), jnp.bfloat16)
    heads_per_core = kv_heads // 2
    factor = math.log2(math.e) / math.sqrt(width)

    def attend(slots, low, high, first=False, last=False):
        @pl.loop(low, high, step=HEADS_AT_ONCE)
        def _(h0):
            items = [(i, p) for i in range(HEADS_AT_ONCE) for p in range(PARTS)]
            part_rows = rows // PARTS
            part_tokens = half_tokens // PARTS

            def scored(i, p):
                h = h0 + i
                at = pl.ds(p * part_rows, part_rows)
                scale_row = kv_heads * (h // heads_per_core) + lax.rem(h, heads_per_core)
                out = []
                for s in slots:
                    k = kvf[s, 0, pl.ds(h, block, stride=kv_heads), :].astype(jnp.bfloat16)
                    raw = lax.dot_general(
                        qs[h, at], k, (((1,), (1,)), ((), ())), preferred_element_type=jnp.float32
                    )
                    key_scale = scf[s, pl.ds(scale_row, 1), :] * factor
                    out.append(raw * key_scale + bias[s, at])
                return out

            def topped(i, p, scores):
                h = h0 + i
                at = pl.ds(p * part_rows, part_rows)
                high_score = scores[0]
                for more in scores[1:]:
                    high_score = jnp.maximum(high_score, more)
                new_top = jnp.broadcast_to(
                    jnp.max(high_score, axis=1, keepdims=True), (part_rows, width)
                )
                old = None
                if not first:
                    old = top[h, at]
                    new_top = jnp.maximum(new_top, old)
                if not last:
                    top[h, at] = new_top
                return old, new_top, [jnp.exp2(z - new_top).astype(jnp.bfloat16) for z in scores]

            def added_up(i, p, found):
                h = h0 + i
                at = pl.ds(p * part_rows, part_rows)
                scale_row = kv_heads * (h // heads_per_core) + lax.rem(h, heads_per_core)
                old, new_top, expos = found
                sums = summed = None
                if not first:
                    shrink = jnp.exp2(old - new_top)
                    sums = total[h, at] * shrink
                    summed = acc[h, at] * shrink
                for s, expo in zip(slots, expos):
                    v = kvf[s, 1, pl.ds(h, block, stride=kv_heads), :].astype(jnp.bfloat16)
                    both = jnp.dot(
                        expo, jnp.concatenate([v, ones], axis=1), preferred_element_type=jnp.float32
                    )
                    value_scale = scf[s, pl.ds(scale_row + heads_per_core, 1), :]
                    added = both[:, :width] * value_scale
                    summed = added if summed is None else summed + added
                    sums = both[:, width:] if sums is None else sums + both[:, width:]
                if last:
                    tokens = pl.ds(p * part_tokens, part_tokens)
                    o_ref[tokens, h] = (
                        (summed / sums).reshape(part_tokens, group, width).astype(o_ref.dtype)
                    )
                else:
                    total[h, at] = sums
                    acc[h, at] = summed

            scores, found = {}, {}
            for n in range(len(items) + 2):
                if n < len(items):
                    scores[n] = scored(*items[n])
                if 0 <= n - 1 < len(items):
                    found[n - 1] = topped(*items[n - 1], scores.pop(n - 1))
                if 0 <= n - 2:
                    added_up(*items[n - 2], found.pop(n - 2))

    lengths = jnp.broadcast_to(len_ref[...].astype(jnp.float32), (8, len_ref.shape[1]))
    docs = len_ref.shape[1]
    upto = lax.broadcasted_iota(jnp.int32, (docs, docs), 0) <= lax.broadcasted_iota(
        jnp.int32, (docs, docs), 1
    )
    ends = jnp.dot(
        lengths, upto.astype(jnp.float32), precision=lax.Precision.HIGHEST,
        preferred_element_type=jnp.float32,
    )[0:1, :]
    offset = lax.broadcasted_iota(jnp.int32, (rows, docs), 0) // group
    here = (ctx * block + c * half_tokens + offset).astype(jnp.float32)
    start = jnp.max(jnp.where(ends <= here, ends, 0.0), axis=1, keepdims=True)
    lane = lax.broadcasted_iota(jnp.int32, (rows, block), 1)
    position = (
        ctx * block + c * half_tokens + lax.broadcasted_iota(jnp.int32, (rows, block), 0) // group
    ).astype(jnp.float32)
    for s in range(5):
        key_position = (ctx * block - s * block + lane).astype(jnp.float32)
        allowed = (key_position >= start) & (key_position <= position)
        bias[s] = jnp.where(allowed, 0.0, MASKED)

    q_copy.wait()

    @pl.loop(0, kv_heads)
    def _(h):
        qs[h] = qb[:, h].astype(jnp.float32).reshape(rows, width).astype(jnp.bfloat16)

    middle = kv_heads // 2
    other_half(0)
    unpack(0)
    came_in(0.0, 3.5)
    attend([0], 0, middle, first=True)
    came_in(3.5, 5.0)
    attend([0], middle, kv_heads, first=True)
    came_in(5.0, 7.3)
    other_half(4)
    unpack(4)
    attend([4], 0, middle)
    came_in(7.3, 8.7)
    attend([4], middle, kv_heads)
    came_in(8.7, 10.3)
    other_half(1)
    other_half(3)
    unpack(1)
    unpack(3)
    attend([1, 3], 0, middle)
    came_in(10.3, 12.0)
    attend([1, 3], middle, kv_heads)
    came_in(12.0, 99.0)
    other_half(2)
    unpack(2)
    attend([2], 0, kv_heads, last=True)

    for sent in open_common:
        outgoing(*sent).wait_send()
    for r in range(COLUMNS):

        @pl.when(x == r)
        def _(r=r):
            for sent in open_role[r]:
                outgoing(*sent).wait_send()


def shards(
    queries, rotated_key_rows, unscaled_value_rows, key_block_scales, value_block_scales, doc_lengths
):
    tokens, heads, width = queries.shape
    kv_heads = rotated_key_rows.shape[1]
    group = heads // kv_heads
    rows = tokens * group
    scales = jnp.concatenate([key_block_scales, value_block_scales], axis=1)
    scales = jnp.broadcast_to(scales[:, :, None], (1, kv_heads, width))
    any_space = pl.BlockSpec(memory_space=pltpu.HBM)
    vmem = pl.BlockSpec(memory_space=pltpu.VMEM)
    out = pl.pallas_call(
        kernel,
        out_shape=jax.ShapeDtypeStruct((tokens, kv_heads, group, width), jnp.bfloat16),
        in_specs=[any_space] * 4 + [vmem],
        out_specs=vmem,
        scratch_shapes=[
            pltpu.VMEM((6, 2, 2 * tokens + 1, kv_heads, width), jnp.bfloat16),
            pltpu.VMEM((tokens, kv_heads, group, width), jnp.bfloat16),
            pltpu.VMEM((kv_heads, rows, width), jnp.bfloat16),
            pltpu.VMEM((5, 2, 2 * tokens * kv_heads, width), jnp.float32),
            pltpu.VMEM((5, 2 * kv_heads, width), jnp.float32),
            pltpu.VMEM((5, rows, 2 * tokens), jnp.float32),
            pltpu.VMEM((kv_heads, rows, width), jnp.float32),
            pltpu.VMEM((kv_heads, rows, width), jnp.float32),
            pltpu.VMEM((kv_heads, rows, width), jnp.float32),
            pltpu.SemaphoreType.DMA((2 + 2 * CHUNKS,)),
            pltpu.SemaphoreType.DMA((100,)),
            pltpu.SemaphoreType.DMA((6, CHUNKS)),
            pltpu.SemaphoreType.DMA((5, CHUNKS)),
        ],
        compiler_params=pltpu.CompilerParams(
            collective_id=0, has_side_effects=True, vmem_limit_bytes=24 * 1024 * 1024
        ),
    )(
        queries.reshape(tokens, kv_heads, group, width),
        rotated_key_rows,
        unscaled_value_rows,
        scales,
        doc_lengths.reshape(1, -1),
    )
    return out.reshape(tokens, heads, width)


def solution(mesh):
    return jax.shard_map(
        shards,
        mesh=mesh,
        in_specs=(
            P(("ctx", "tp"), None, None),
            P(("ctx", "tp"), None, None),
            P(("ctx", "tp"), None, None),
            P("ctx", "tp"),
            P("ctx", "tp"),
            P(),
        ),
        out_specs=P(("ctx", "tp"), None, None),
        check_vma=False,
    )
```

```python
import math

import jax
import jax.numpy as jnp
from jax import lax
from jax.experimental import pallas as pl
from jax.experimental.pallas import tpu as pltpu
from jax.sharding import PartitionSpec as P

CHUNKS = 4
COLUMNS = 4
MASKED = -1e30
HEADS_AT_ONCE = 2
PARTS = 1


def relays(role, slot, chunk):
    early = chunk < CHUNKS // 2
    out = []
    if slot == 4:
        if role in (2, 3) or (role == 1 and early):
            out.append(("left", 3))
        if role == 3:
            out.append(("right", 1))
    if slot == 1:
        if early and role in (0, 1, 2):
            out.append(("right", 2))
        if role == 3 and not early:
            out.append(("next_row", 5))
    if slot == 3:
        if (role == 1 and early) or (role in (2, 3) and not early):
            out.append(("left", 2))
    if slot == 5:
        if role == 0:
            out.extend([("left", 2), ("next_row", 3)])
        if role == 3:
            out.append(("right", 2))
    return out


def first_sends(role, chunk):
    out = []
    if role == 0:
        out.append(("left", 3))
    if role == 1 and chunk >= CHUNKS // 2:
        out.append(("left", 5))
    if role in (0, 1, 2):
        out.append(("right", 1))
    return out


EARLY = [3.0, 4.4, 5.8, 7.2]
EXPECTED = {
    0: {4: EARLY, 5: [None, None, 3.0, 4.4], 3: [6.0, 7.4, 8.6, 10.0], 1: [6.0, 7.4, 8.8, 10.2],
        2: [9.0, 10.4, 11.8, 13.2]},
    1: {4: EARLY, 1: EARLY, 3: [6.0, 7.4, 8.8, 10.2], 2: [9.0, 10.4, 11.8, 13.2]},
    2: {4: EARLY, 1: EARLY, 3: [6.0, 7.4, 8.8, 10.2], 2: [8.6, 10.0, 11.6, 13.0]},
    3: {4: EARLY, 1: EARLY, 3: EARLY, 5: [None, None, 8.8, 10.2], 2: [8.6, 10.0, 8.6, 10.0]},
}


def kernel(
    q_hbm, k_hbm, v_hbm, sc_hbm, len_hbm, o_ref,
    len_ref, kvb, qb, qs, kvf, scf, bias, top, total, acc,
    lsem, ssem, rsem, fsem,
):
    ctx, c = lax.axis_index("ctx"), lax.axis_index("tp")
    count = lax.axis_size("ctx")
    x = lax.rem(ctx, COLUMNS)
    row = ctx - x
    half_tokens, kv_heads, group, width = qb.shape[0], qb.shape[1], qb.shape[2], qb.shape[3]
    block = 2 * half_tokens
    piece = half_tokens // CHUNKS
    rows = half_tokens * group
    where = {
        "partner": (ctx, 1 - c),
        "right": (row + lax.rem(x + 1, COLUMNS), c),
        "left": (row + lax.rem(x + COLUMNS - 1, COLUMNS), c),
        "next_row": (lax.rem(ctx + COLUMNS, count), c),
    }
    last_row = (lax.rem(ctx + count - COLUMNS, count), c)

    def part(slot, half, j):
        if j == 0:
            return kvb.at[slot, half, pl.ds(0, 2 * piece + 1)]
        return kvb.at[slot, half, pl.ds(1 + 2 * piece * j, 2 * piece)]

    staged = [[] for _ in range(CHUNKS)]
    staged[0].append(pltpu.make_async_copy(sc_hbm, kvb.at[0, c, pl.ds(0, 1)], lsem.at[0]))
    for j in range(CHUNKS):
        at = 1 + 2 * piece * j
        source = pl.ds(piece * j, piece)
        staged[j].append(
            pltpu.make_async_copy(k_hbm.at[source], kvb.at[0, c, pl.ds(at, piece)], lsem.at[1 + 2 * j])
        )
        staged[j].append(
            pltpu.make_async_copy(
                v_hbm.at[source], kvb.at[0, c, pl.ds(at + piece, piece)], lsem.at[2 + 2 * j]
            )
        )
    for copies in staged:
        for copy in copies:
            copy.start()
    q_copy = pltpu.make_async_copy(q_hbm, qb, lsem.at[1 + 2 * CHUNKS])
    q_copy.start()
    len_copy = pltpu.make_async_copy(len_hbm, len_ref, lsem.at[2 + 2 * CHUNKS])
    len_copy.start()

    barrier = pltpu.get_barrier_semaphore()
    others = list(where.values()) + [last_row]
    for other in others:
        pl.semaphore_signal(barrier, inc=1, device_id=other, device_id_type=pl.DeviceIdType.MESH)
    pl.semaphore_wait(barrier, len(others))

    counter = [0]
    open_common = []
    open_role = {r: [] for r in range(COLUMNS)}

    def remote(src, dst, send, recv, to):
        return pltpu.make_async_remote_copy(
            src_ref=src, dst_ref=dst, send_sem=ssem.at[send], recv_sem=recv,
            device_id=where[to], device_id_type=pl.DeviceIdType.MESH,
        )

    def outgoing(slot, j, to, there, number):
        recv = fsem.at[there, j] if to == "partner" else rsem.at[there, j]
        return remote(part(slot, c, j), part(there, c, j), number, recv, to)

    def send(slot, j, to, there, opened):
        sent = (slot, j, to, there, counter[0])
        counter[0] += 1
        outgoing(*sent).start()
        opened.append(sent)

    for j in range(CHUNKS):
        for copy in staged[j]:
            copy.wait()
        send(0, j, "next_row", 4, open_common)
        after_common = counter[0]
        for r in range(COLUMNS):
            counter[0] = after_common

            @pl.when(x == r)
            def _(r=r, j=j):
                for to, there in first_sends(r, j):
                    send(0, j, to, there, open_role[r])

        counter[0] = after_common + 2
        send(0, j, "partner", 0, open_common)

    order = {}
    for r in range(COLUMNS):
        events = [
            (times[j], slot, j)
            for slot, times in EXPECTED[r].items()
            for j in range(CHUNKS)
            if times[j] is not None
        ]
        order[r] = sorted(events)

    def came_in(since, until):
        first = counter[0]
        most = first
        for r in range(COLUMNS):
            counter[0] = first

            @pl.when(x == r)
            def _(r=r):
                for time, slot, j in order[r]:
                    if not since <= time < until:
                        continue
                    there = part(slot, c, j)
                    remote(there, there, 0, rsem.at[slot, j], "partner").wait_recv()
                    for to, target in relays(r, slot, j):
                        send(slot, j, to, target, open_role[r])
                    if slot != 5:
                        send(slot, j, "partner", slot, open_role[r])

            most = max(most, counter[0])
        counter[0] = most

    def other_half(slot):
        for j in range(CHUNKS):
            there = part(slot, 1 - c, j)
            remote(there, there, 0, fsem.at[slot, j], "partner").wait_recv()

    def unpack(slot):
        for half in range(2):
            scf[slot, pl.ds(kv_heads * half, kv_heads), :] = kvb[slot, half, 0].astype(jnp.float32)
            for j in range(CHUNKS):
                at = 1 + 2 * piece * j
                to = pl.ds((half_tokens * half + piece * j) * kv_heads, piece * kv_heads)
                for which in range(2):
                    tile = kvb[slot, half, pl.ds(at + which * piece, piece)].astype(jnp.float32)
                    kvf[slot, which, to, :] = tile.reshape(piece * kv_heads, width)

    ones = jnp.ones((block, width), jnp.bfloat16)
    heads_per_core = kv_heads // 2
    factor = math.log2(math.e) / math.sqrt(width)

    def attend(slots, low, high, first=False, last=False):
        @pl.loop(low, high, step=HEADS_AT_ONCE)
        def _(h0):
            items = [(i, p) for i in range(HEADS_AT_ONCE) for p in range(PARTS)]
            part_rows = rows // PARTS
            part_tokens = half_tokens // PARTS

            def scored(i, p):
                h = h0 + i
                at = pl.ds(p * part_rows, part_rows)
                scale_row = kv_heads * (h // heads_per_core) + lax.rem(h, heads_per_core)
                out = []
                for s in slots:
                    k = kvf[s, 0, pl.ds(h, block, stride=kv_heads), :].astype(jnp.bfloat16)
                    raw = lax.dot_general(
                        qs[h, at], k, (((1,), (1,)), ((), ())), preferred_element_type=jnp.float32
                    )
                    key_scale = scf[s, pl.ds(scale_row, 1), :] * factor
                    out.append(raw * key_scale + bias[s, at])
                return out

            def topped(i, p, scores):
                h = h0 + i
                at = pl.ds(p * part_rows, part_rows)
                high_score = scores[0]
                for more in scores[1:]:
                    high_score = jnp.maximum(high_score, more)
                new_top = jnp.broadcast_to(
                    jnp.max(high_score, axis=1, keepdims=True), (part_rows, width)
                )
                old = None
                if not first:
                    old = top[h, at]
                    new_top = jnp.maximum(new_top, old)
                if not last:
                    top[h, at] = new_top
                return old, new_top, [jnp.exp2(z - new_top).astype(jnp.bfloat16) for z in scores]

            def added_up(i, p, found):
                h = h0 + i
                at = pl.ds(p * part_rows, part_rows)
                scale_row = kv_heads * (h // heads_per_core) + lax.rem(h, heads_per_core)
                old, new_top, expos = found
                sums = summed = None
                if not first:
                    shrink = jnp.exp2(old - new_top)
                    sums = total[h, at] * shrink
                    summed = acc[h, at] * shrink
                for s, expo in zip(slots, expos):
                    v = kvf[s, 1, pl.ds(h, block, stride=kv_heads), :].astype(jnp.bfloat16)
                    both = jnp.dot(
                        expo, jnp.concatenate([v, ones], axis=1), preferred_element_type=jnp.float32
                    )
                    value_scale = scf[s, pl.ds(scale_row + heads_per_core, 1), :]
                    added = both[:, :width] * value_scale
                    summed = added if summed is None else summed + added
                    sums = both[:, width:] if sums is None else sums + both[:, width:]
                if last:
                    tokens = pl.ds(p * part_tokens, part_tokens)
                    o_ref[tokens, h] = (
                        (summed / sums).reshape(part_tokens, group, width).astype(o_ref.dtype)
                    )
                else:
                    total[h, at] = sums
                    acc[h, at] = summed

            scores, found = {}, {}
            for n in range(len(items) + 2):
                if n < len(items):
                    scores[n] = scored(*items[n])
                if 0 <= n - 1 < len(items):
                    found[n - 1] = topped(*items[n - 1], scores.pop(n - 1))
                if 0 <= n - 2:
                    added_up(*items[n - 2], found.pop(n - 2))

    len_copy.wait()
    lengths = jnp.broadcast_to(len_ref[...].astype(jnp.float32), (8, len_ref.shape[1]))
    docs = len_ref.shape[1]
    upto = lax.broadcasted_iota(jnp.int32, (docs, docs), 0) <= lax.broadcasted_iota(
        jnp.int32, (docs, docs), 1
    )
    ends = jnp.dot(
        lengths, upto.astype(jnp.float32), precision=lax.Precision.HIGHEST,
        preferred_element_type=jnp.float32,
    )[0:1, :]
    offset = lax.broadcasted_iota(jnp.int32, (rows, docs), 0) // group
    here = (ctx * block + c * half_tokens + offset).astype(jnp.float32)
    start = jnp.max(jnp.where(ends <= here, ends, 0.0), axis=1, keepdims=True)
    lane = lax.broadcasted_iota(jnp.int32, (rows, block), 1)
    position = (
        ctx * block + c * half_tokens + lax.broadcasted_iota(jnp.int32, (rows, block), 0) // group
    ).astype(jnp.float32)
    for s in range(5):
        key_position = (ctx * block - s * block + lane).astype(jnp.float32)
        allowed = (key_position >= start) & (key_position <= position)
        bias[s] = jnp.where(allowed, 0.0, MASKED)

    q_copy.wait()

    @pl.loop(0, kv_heads)
    def _(h):
        qs[h] = qb[:, h].astype(jnp.float32).reshape(rows, width).astype(jnp.bfloat16)

    middle = kv_heads // 2
    other_half(0)
    unpack(0)
    came_in(0.0, 3.5)
    attend([0], 0, middle, first=True)
    came_in(3.5, 5.0)
    attend([0], middle, kv_heads, first=True)
    came_in(5.0, 7.3)
    other_half(4)
    unpack(4)
    attend([4], 0, middle)
    came_in(7.3, 8.7)
    attend([4], middle, kv_heads)
    came_in(8.7, 10.3)
    other_half(1)
    other_half(3)
    unpack(1)
    unpack(3)
    attend([1, 3], 0, middle)
    came_in(10.3, 12.0)
    attend([1, 3], middle, kv_heads)
    came_in(12.0, 99.0)
    other_half(2)
    unpack(2)
    attend([2], 0, kv_heads, last=True)

    for sent in open_common:
        outgoing(*sent).wait_send()
    for r in range(COLUMNS):

        @pl.when(x == r)
        def _(r=r):
            for sent in open_role[r]:
                outgoing(*sent).wait_send()


def shards(
    queries, rotated_key_rows, unscaled_value_rows, key_block_scales, value_block_scales, doc_lengths
):
    tokens, heads, width = queries.shape
    kv_heads = rotated_key_rows.shape[1]
    group = heads // kv_heads
    rows = tokens * group
    scales = jnp.concatenate([key_block_scales, value_block_scales], axis=1)
    scales = jnp.broadcast_to(scales[:, :, None], (1, kv_heads, width))
    in_place = pl.BlockSpec(memory_space=pltpu.HBM)
    vmem = pl.BlockSpec(memory_space=pltpu.VMEM)
    out = pl.pallas_call(
        kernel,
        out_shape=jax.ShapeDtypeStruct((tokens, kv_heads, group, width), jnp.bfloat16),
        in_specs=[in_place] * 5,
        out_specs=vmem,
        scratch_shapes=[
            pltpu.VMEM((1, doc_lengths.shape[0]), jnp.int32),
            pltpu.VMEM((6, 2, 2 * tokens + 1, kv_heads, width), jnp.bfloat16),
            pltpu.VMEM((tokens, kv_heads, group, width), jnp.bfloat16),
            pltpu.VMEM((kv_heads, rows, width), jnp.bfloat16),
            pltpu.VMEM((5, 2, 2 * tokens * kv_heads, width), jnp.float32),
            pltpu.VMEM((5, 2 * kv_heads, width), jnp.float32),
            pltpu.VMEM((5, rows, 2 * tokens), jnp.float32),
            pltpu.VMEM((kv_heads, rows, width), jnp.float32),
            pltpu.VMEM((kv_heads, rows, width), jnp.float32),
            pltpu.VMEM((kv_heads, rows, width), jnp.float32),
            pltpu.SemaphoreType.DMA((3 + 2 * CHUNKS,)),
            pltpu.SemaphoreType.DMA((100,)),
            pltpu.SemaphoreType.DMA((6, CHUNKS)),
            pltpu.SemaphoreType.DMA((5, CHUNKS)),
        ],
        compiler_params=pltpu.CompilerParams(
            collective_id=0, has_side_effects=True, vmem_limit_bytes=24 * 1024 * 1024
        ),
    )(
        pltpu.with_memory_space_constraint(queries.reshape(tokens, kv_heads, group, width), pltpu.HBM),
        pltpu.with_memory_space_constraint(rotated_key_rows, pltpu.HBM),
        pltpu.with_memory_space_constraint(unscaled_value_rows, pltpu.HBM),
        scales,
        pltpu.with_memory_space_constraint(doc_lengths.reshape(1, -1), pltpu.HBM),
    )
    return out.reshape(tokens, heads, width)


def solution(mesh):
    return jax.shard_map(
        shards,
        mesh=mesh,
        in_specs=(
            P(("ctx", "tp"), None, None),
            P(("ctx", "tp"), None, None),
            P(("ctx", "tp"), None, None),
            P("ctx", "tp"),
            P("ctx", "tp"),
            P(),
        ),
        out_specs=P(("ctx", "tp"), None, None),
        check_vma=False,
    )
```

```python
import math

import jax
import jax.numpy as jnp
from jax import lax
from jax.experimental import pallas as pl
from jax.experimental.pallas import tpu as pltpu
from jax.sharding import PartitionSpec as P

CHUNKS = 4
COLUMNS = 4
MASKED = -1e30
HEADS_AT_ONCE = 2


def relays(role, slot, chunk):
    early = chunk < CHUNKS // 2
    out = []
    if slot == 4:
        if role in (2, 3) or (role == 1 and early):
            out.append(("left", 3))
        if role == 3:
            out.append(("right", 1))
    if slot == 1:
        if early and role in (0, 1, 2):
            out.append(("right", 2))
        if role == 3 and not early:
            out.append(("next_row", 5))
    if slot == 3:
        if (role == 1 and early) or (role in (2, 3) and not early):
            out.append(("left", 2))
    if slot == 5:
        if role == 0:
            out.extend([("left", 2), ("next_row", 3)])
        if role == 3:
            out.append(("right", 2))
    return out


def first_sends(role, chunk):
    out = []
    if role == 0:
        out.append(("left", 3))
    if role == 1 and chunk >= CHUNKS // 2:
        out.append(("left", 5))
    if role in (0, 1, 2):
        out.append(("right", 1))
    return out


EARLY = [3.0, 4.4, 5.8, 7.2]
EXPECTED = {
    0: {4: EARLY, 5: [None, None, 3.0, 4.4], 3: [6.0, 7.4, 8.6, 10.0], 1: [6.0, 7.4, 8.8, 10.2],
        2: [9.0, 10.4, 11.8, 13.2]},
    1: {4: EARLY, 1: EARLY, 3: [6.0, 7.4, 8.8, 10.2], 2: [9.0, 10.4, 11.8, 13.2]},
    2: {4: EARLY, 1: EARLY, 3: [6.0, 7.4, 8.8, 10.2], 2: [8.6, 10.0, 11.6, 13.0]},
    3: {4: EARLY, 1: EARLY, 3: EARLY, 5: [None, None, 8.8, 10.2], 2: [8.6, 10.0, 8.6, 10.0]},
}


def kernel(
    q_hbm, k_hbm, v_hbm, sc_hbm, len_hbm, o_ref,
    len_ref, kvb, qb, qs, kvf, scf, bias, top, total, acc,
    lsem, ssem, rsem, fsem,
):
    ctx, c = lax.axis_index("ctx"), lax.axis_index("tp")
    count = lax.axis_size("ctx")
    x = lax.rem(ctx, COLUMNS)
    row = ctx - x
    half_tokens, kv_heads, group, width = qb.shape[0], qb.shape[1], qb.shape[2], qb.shape[3]
    block = 2 * half_tokens
    piece = half_tokens // CHUNKS
    rows = half_tokens * group
    where = {
        "partner": (ctx, 1 - c),
        "right": (row + lax.rem(x + 1, COLUMNS), c),
        "left": (row + lax.rem(x + COLUMNS - 1, COLUMNS), c),
        "next_row": (lax.rem(ctx + COLUMNS, count), c),
    }
    last_row = (lax.rem(ctx + count - COLUMNS, count), c)

    def part(slot, half, j):
        if j == 0:
            return kvb.at[slot, half, pl.ds(0, 2 * piece + 1)]
        return kvb.at[slot, half, pl.ds(1 + 2 * piece * j, 2 * piece)]

    staged = [[] for _ in range(CHUNKS)]
    staged[0].append(pltpu.make_async_copy(sc_hbm, kvb.at[0, c, pl.ds(0, 1)], lsem.at[0]))
    for j in range(CHUNKS):
        at = 1 + 2 * piece * j
        source = pl.ds(piece * j, piece)
        staged[j].append(
            pltpu.make_async_copy(k_hbm.at[source], kvb.at[0, c, pl.ds(at, piece)], lsem.at[1 + 2 * j])
        )
        staged[j].append(
            pltpu.make_async_copy(
                v_hbm.at[source], kvb.at[0, c, pl.ds(at + piece, piece)], lsem.at[2 + 2 * j]
            )
        )
    for copies in staged:
        for copy in copies:
            copy.start()
    q_copy = pltpu.make_async_copy(q_hbm, qb, lsem.at[1 + 2 * CHUNKS])
    q_copy.start()
    len_copy = pltpu.make_async_copy(len_hbm, len_ref, lsem.at[2 + 2 * CHUNKS])
    len_copy.start()

    barrier = pltpu.get_barrier_semaphore()
    others = list(where.values()) + [last_row]
    for other in others:
        pl.semaphore_signal(barrier, inc=1, device_id=other, device_id_type=pl.DeviceIdType.MESH)
    pl.semaphore_wait(barrier, len(others))

    counter = [0]
    open_common = []
    open_role = {r: [] for r in range(COLUMNS)}

    def remote(src, dst, send, recv, to):
        return pltpu.make_async_remote_copy(
            src_ref=src, dst_ref=dst, send_sem=ssem.at[send], recv_sem=recv,
            device_id=where[to], device_id_type=pl.DeviceIdType.MESH,
        )

    def outgoing(slot, j, to, there, number):
        recv = fsem.at[there, j] if to == "partner" else rsem.at[there, j]
        return remote(part(slot, c, j), part(there, c, j), number, recv, to)

    def send(slot, j, to, there, opened):
        sent = (slot, j, to, there, counter[0])
        counter[0] += 1
        outgoing(*sent).start()
        opened.append(sent)

    for j in range(CHUNKS):
        for copy in staged[j]:
            copy.wait()
        send(0, j, "next_row", 4, open_common)
        after_common = counter[0]
        for r in range(COLUMNS):
            counter[0] = after_common

            @pl.when(x == r)
            def _(r=r, j=j):
                for to, there in first_sends(r, j):
                    send(0, j, to, there, open_role[r])

        counter[0] = after_common + 2
        send(0, j, "partner", 0, open_common)

    order = {}
    for r in range(COLUMNS):
        events = [
            (times[j], slot, j)
            for slot, times in EXPECTED[r].items()
            for j in range(CHUNKS)
            if times[j] is not None
        ]
        order[r] = sorted(events)

    def came_in(since, until):
        first = counter[0]
        most = first
        for r in range(COLUMNS):
            counter[0] = first

            @pl.when(x == r)
            def _(r=r):
                for time, slot, j in order[r]:
                    if not since <= time < until:
                        continue
                    there = part(slot, c, j)
                    remote(there, there, 0, rsem.at[slot, j], "partner").wait_recv()
                    for to, target in relays(r, slot, j):
                        send(slot, j, to, target, open_role[r])
                    if slot != 5:
                        send(slot, j, "partner", slot, open_role[r])

            most = max(most, counter[0])
        counter[0] = most

    def other_half(slot):
        for j in range(CHUNKS):
            there = part(slot, 1 - c, j)
            remote(there, there, 0, fsem.at[slot, j], "partner").wait_recv()

    def unpack(slot):
        for half in range(2):
            scf[slot, pl.ds(kv_heads * half, kv_heads), :] = kvb[slot, half, 0].astype(jnp.float32)
            for j in range(CHUNKS):
                at = 1 + 2 * piece * j
                to = pl.ds((half_tokens * half + piece * j) * kv_heads, piece * kv_heads)
                for which in range(2):
                    tile = kvb[slot, half, pl.ds(at + which * piece, piece)].astype(jnp.float32)
                    kvf[slot, which, to, :] = tile.reshape(piece * kv_heads, width)

    heads_per_core = kv_heads // 2
    factor = math.log2(math.e) / math.sqrt(width)

    def attend(slots, before, low, high, last=False):
        first = before is None

        @pl.loop(low, high, step=HEADS_AT_ONCE)
        def _(h0):
            def scale(s, h, which):
                at = kv_heads * (h // heads_per_core) + lax.rem(h, heads_per_core)
                one = scf[s, pl.ds(at + which * heads_per_core, 1), :]
                return jnp.concatenate([one] * (rows // width), axis=1)

            def scored(i):
                h = h0 + i
                out = []
                for s in slots:
                    k = kvf[s, 0, pl.ds(h, block, stride=kv_heads), :].astype(jnp.bfloat16)
                    raw = jnp.dot(k, qs[h], preferred_element_type=jnp.float32)
                    out.append(raw * (scale(s, h, 0) * factor) + bias[s])
                return out

            def topped(i, scores):
                h = h0 + i
                high_score = scores[0]
                for more in scores[1:]:
                    high_score = jnp.maximum(high_score, more)
                new_top = jnp.max(high_score, axis=0, keepdims=True)
                sums = shrink = None
                if not first:
                    old = top[h]
                    new_top = jnp.maximum(new_top, old)
                    shrink = jnp.exp2(old - new_top)
                    sums = total[h] * shrink
                if not last:
                    top[h] = new_top
                expos = []
                for score in scores:
                    expo = jnp.exp2(score - new_top)
                    added = jnp.sum(expo, axis=0, keepdims=True)
                    sums = added if sums is None else sums + added
                    expos.append(expo.astype(jnp.bfloat16))
                return sums, shrink, expos

            def added_up(i, found):
                h = h0 + i
                sums, shrink, expos = found
                summed = None if first else acc[h]
                unit = None if first else scale(before, h, 1)
                for s, expo in zip(slots, expos):
                    v = kvf[s, 1, pl.ds(h, block, stride=kv_heads), :].T.astype(jnp.bfloat16)
                    added = jnp.dot(v, expo, preferred_element_type=jnp.float32)
                    new_unit = scale(s, h, 1)
                    if summed is None:
                        summed = added
                    else:
                        ratio = unit / new_unit
                        if shrink is not None:
                            ratio = ratio * shrink
                        summed = summed * ratio + added
                    unit, shrink = new_unit, None
                if last:
                    result = (summed * (unit / sums)).T
                    o_ref[:, h] = result.reshape(half_tokens, group, width).astype(o_ref.dtype)
                else:
                    total[h] = sums
                    acc[h] = summed

            scores, found = {}, {}
            for n in range(HEADS_AT_ONCE + 2):
                if n < HEADS_AT_ONCE:
                    scores[n] = scored(n)
                if 0 <= n - 1 < HEADS_AT_ONCE:
                    found[n - 1] = topped(n - 1, scores.pop(n - 1))
                if 0 <= n - 2:
                    added_up(n - 2, found.pop(n - 2))

    len_copy.wait()
    lengths = jnp.broadcast_to(len_ref[...].astype(jnp.float32), (8, len_ref.shape[1]))
    docs = len_ref.shape[1]
    upto = lax.broadcasted_iota(jnp.int32, (docs, docs), 1) <= lax.broadcasted_iota(
        jnp.int32, (docs, docs), 0
    )
    ends = lax.dot_general(
        upto.astype(jnp.float32), lengths, (((1,), (1,)), ((), ())),
        precision=lax.Precision.HIGHEST, preferred_element_type=jnp.float32,
    )[:, 0:1]
    here = ctx * block + c * half_tokens + lax.broadcasted_iota(jnp.int32, (1, rows), 1) // group
    position = here.astype(jnp.float32)
    start = jnp.max(jnp.where(ends <= position, ends, 0.0), axis=0, keepdims=True)
    for s in range(5):
        key_position = (
            ctx * block - s * block + lax.broadcasted_iota(jnp.int32, (block, rows), 0)
        ).astype(jnp.float32)
        allowed = (key_position >= start) & (key_position <= position)
        bias[s] = jnp.where(allowed, 0.0, MASKED)

    q_copy.wait()

    @pl.loop(0, kv_heads)
    def _(h):
        qs[h] = qb[:, h].astype(jnp.float32).reshape(rows, width).T.astype(jnp.bfloat16)

    middle = kv_heads // 2
    other_half(0)
    unpack(0)
    attend([0], None, 0, middle)
    came_in(0.0, 3.5)
    attend([0], None, middle, kv_heads)
    came_in(3.5, 7.3)
    other_half(4)
    unpack(4)
    attend([4], 0, 0, 2)
    came_in(7.3, 7.5)
    attend([4], 0, 2, 6)
    came_in(7.5, 8.7)
    attend([4], 0, 6, kv_heads)
    came_in(8.7, 10.3)
    other_half(1)
    unpack(1)
    attend([1], 4, 0, middle)
    came_in(10.3, 10.5)
    attend([1], 4, middle, kv_heads)
    other_half(3)
    unpack(3)
    attend([3], 1, 0, middle)
    came_in(10.5, 12.0)
    attend([3], 1, middle, kv_heads)
    came_in(12.0, 99.0)
    other_half(2)
    unpack(2)
    attend([2], 3, 0, kv_heads, last=True)

    for sent in open_common:
        outgoing(*sent).wait_send()
    for r in range(COLUMNS):

        @pl.when(x == r)
        def _(r=r):
            for sent in open_role[r]:
                outgoing(*sent).wait_send()


def shards(
    queries, rotated_key_rows, unscaled_value_rows, key_block_scales, value_block_scales, doc_lengths
):
    tokens, heads, width = queries.shape
    kv_heads = rotated_key_rows.shape[1]
    group = heads // kv_heads
    rows = tokens * group
    scales = jnp.concatenate([key_block_scales, value_block_scales], axis=1)
    scales = jnp.broadcast_to(scales[:, :, None], (1, kv_heads, width))
    in_place = pl.BlockSpec(memory_space=pltpu.HBM)
    vmem = pl.BlockSpec(memory_space=pltpu.VMEM)
    out = pl.pallas_call(
        kernel,
        out_shape=jax.ShapeDtypeStruct((tokens, kv_heads, group, width), jnp.bfloat16),
        in_specs=[in_place] * 5,
        out_specs=vmem,
        scratch_shapes=[
            pltpu.VMEM((1, doc_lengths.shape[0]), jnp.int32),
            pltpu.VMEM((6, 2, 2 * tokens + 1, kv_heads, width), jnp.bfloat16),
            pltpu.VMEM((tokens, kv_heads, group, width), jnp.bfloat16),
            pltpu.VMEM((kv_heads, width, rows), jnp.bfloat16),
            pltpu.VMEM((5, 2, 2 * tokens * kv_heads, width), jnp.float32),
            pltpu.VMEM((5, 2 * kv_heads, width), jnp.float32),
            pltpu.VMEM((5, 2 * tokens, rows), jnp.float32),
            pltpu.VMEM((kv_heads, 1, rows), jnp.float32),
            pltpu.VMEM((kv_heads, 1, rows), jnp.float32),
            pltpu.VMEM((kv_heads, width, rows), jnp.float32),
            pltpu.SemaphoreType.DMA((3 + 2 * CHUNKS,)),
            pltpu.SemaphoreType.DMA((100,)),
            pltpu.SemaphoreType.DMA((6, CHUNKS)),
            pltpu.SemaphoreType.DMA((5, CHUNKS)),
        ],
        compiler_params=pltpu.CompilerParams(
            collective_id=0, has_side_effects=True, vmem_limit_bytes=24 * 1024 * 1024
        ),
    )(
        pltpu.with_memory_space_constraint(queries.reshape(tokens, kv_heads, group, width), pltpu.HBM),
        pltpu.with_memory_space_constraint(rotated_key_rows, pltpu.HBM),
        pltpu.with_memory_space_constraint(unscaled_value_rows, pltpu.HBM),
        scales,
        pltpu.with_memory_space_constraint(doc_lengths.reshape(1, -1), pltpu.HBM),
    )
    return out.reshape(tokens, heads, width)


def solution(mesh):
    return jax.shard_map(
        shards,
        mesh=mesh,
        in_specs=(
            P(("ctx", "tp"), None, None),
            P(("ctx", "tp"), None, None),
            P(("ctx", "tp"), None, None),
            P("ctx", "tp"),
            P("ctx", "tp"),
            P(),
        ),
        out_specs=P(("ctx", "tp"), None, None),
        check_vma=False,
    )
```

```python
import math

import jax
import jax.numpy as jnp
from jax import lax
from jax.experimental import pallas as pl
from jax.experimental.pallas import tpu as pltpu
from jax.sharding import PartitionSpec as P

CHUNKS = 4
COLUMNS = 4
MASKED = -1e30
HEADS_AT_ONCE = 2


def relays(role, slot, chunk):
    early = chunk < CHUNKS // 2
    out = []
    if slot == 4:
        if role in (2, 3) or (role == 1 and early):
            out.append(("left", 3))
        if role == 3:
            out.append(("right", 1))
    if slot == 1:
        if early and role in (0, 1, 2):
            out.append(("right", 2))
        if role == 3 and not early:
            out.append(("next_row", 5))
    if slot == 3:
        if (role == 1 and early) or (role in (2, 3) and not early):
            out.append(("left", 2))
    if slot == 5:
        if role == 0:
            out.extend([("left", 2), ("next_row", 3)])
        if role == 3:
            out.append(("right", 2))
    return out


def first_sends(role, chunk):
    out = []
    if role == 0:
        out.append(("left", 3))
    if role == 1 and chunk >= CHUNKS // 2:
        out.append(("left", 5))
    if role in (0, 1, 2):
        out.append(("right", 1))
    return out


EARLY = [3.0, 4.4, 5.8, 7.2]
EXPECTED = {
    0: {4: EARLY, 5: [None, None, 3.0, 4.4], 3: [6.0, 7.4, 8.6, 10.0], 1: [6.0, 7.4, 8.8, 10.2],
        2: [9.0, 10.4, 11.8, 13.2]},
    1: {4: EARLY, 1: EARLY, 3: [6.0, 7.4, 8.8, 10.2], 2: [9.0, 10.4, 11.8, 13.2]},
    2: {4: EARLY, 1: EARLY, 3: [6.0, 7.4, 8.8, 10.2], 2: [8.6, 10.0, 11.6, 13.0]},
    3: {4: EARLY, 1: EARLY, 3: EARLY, 5: [None, None, 8.8, 10.2], 2: [8.6, 10.0, 8.6, 10.0]},
}


def kernel(
    q_hbm, k_hbm, v_hbm, sc_hbm, len_hbm, o_ref,
    len_ref, kvb, qb, qs, kvf, scf, bias, top, total, acc,
    lsem, ssem, rsem, fsem,
):
    ctx, c = lax.axis_index("ctx"), lax.axis_index("tp")
    count = lax.axis_size("ctx")
    x = lax.rem(ctx, COLUMNS)
    row = ctx - x
    half_tokens, kv_heads, group, width = qb.shape[0], qb.shape[1], qb.shape[2], qb.shape[3]
    block = 2 * half_tokens
    piece = half_tokens // CHUNKS
    rows = half_tokens * group
    where = {
        "partner": (ctx, 1 - c),
        "right": (row + lax.rem(x + 1, COLUMNS), c),
        "left": (row + lax.rem(x + COLUMNS - 1, COLUMNS), c),
        "next_row": (lax.rem(ctx + COLUMNS, count), c),
    }
    last_row = (lax.rem(ctx + count - COLUMNS, count), c)

    def part(slot, half, j):
        if j == 0:
            return kvb.at[slot, half, pl.ds(0, 2 * piece + 1)]
        return kvb.at[slot, half, pl.ds(1 + 2 * piece * j, 2 * piece)]

    staged = [[] for _ in range(CHUNKS)]
    staged[0].append(pltpu.make_async_copy(sc_hbm, kvb.at[0, c, pl.ds(0, 1)], lsem.at[0]))
    for j in range(CHUNKS):
        at = 1 + 2 * piece * j
        source = pl.ds(piece * j, piece)
        staged[j].append(
            pltpu.make_async_copy(k_hbm.at[source], kvb.at[0, c, pl.ds(at, piece)], lsem.at[1 + 2 * j])
        )
        staged[j].append(
            pltpu.make_async_copy(
                v_hbm.at[source], kvb.at[0, c, pl.ds(at + piece, piece)], lsem.at[2 + 2 * j]
            )
        )
    for copies in staged:
        for copy in copies:
            copy.start()
    q_copy = pltpu.make_async_copy(q_hbm, qb, lsem.at[1 + 2 * CHUNKS])
    q_copy.start()
    len_copy = pltpu.make_async_copy(len_hbm, len_ref, lsem.at[2 + 2 * CHUNKS])
    len_copy.start()

    barrier = pltpu.get_barrier_semaphore()
    has_next = ctx < count - COLUMNS
    has_last = ctx >= COLUMNS

    def greet(other):
        pl.semaphore_signal(barrier, inc=1, device_id=other, device_id_type=pl.DeviceIdType.MESH)

    for other in ("partner", "right", "left"):
        greet(where[other])
    pl.when(has_next)(lambda: greet(where["next_row"]))
    pl.when(has_last)(lambda: greet(last_row))

    def stand_in(slot, chunks):
        for j in chunks:
            at = 1 + 2 * piece * j
            source = pl.ds(piece * j, piece)
            sem = rsem.at[slot, j]
            if j == 0:
                pltpu.make_async_copy(sc_hbm, kvb.at[slot, c, pl.ds(0, 1)], sem).start()
            pltpu.make_async_copy(k_hbm.at[source], kvb.at[slot, c, pl.ds(at, piece)], sem).start()
            pltpu.make_async_copy(
                v_hbm.at[source], kvb.at[slot, c, pl.ds(at + piece, piece)], sem
            ).start()

    late = range(CHUNKS // 2, CHUNKS)
    pl.when(jnp.logical_not(has_last))(lambda: stand_in(4, range(CHUNKS)))
    pl.when(ctx == 0)(lambda: stand_in(3, late))
    pl.when(ctx == COLUMNS - 1)(lambda: stand_in(5, late))
    pl.semaphore_wait(barrier, 3 + has_next.astype(jnp.int32) + has_last.astype(jnp.int32))

    counter = [0]
    open_common = []
    open_role = {r: [] for r in range(COLUMNS)}

    def remote(src, dst, send, recv, to):
        return pltpu.make_async_remote_copy(
            src_ref=src, dst_ref=dst, send_sem=ssem.at[send], recv_sem=recv,
            device_id=where[to], device_id_type=pl.DeviceIdType.MESH,
        )

    def outgoing(slot, j, to, there, number):
        recv = fsem.at[there, j] if to == "partner" else rsem.at[there, j]
        return remote(part(slot, c, j), part(there, c, j), number, recv, to)

    def send(slot, j, to, there, opened):
        sent = (slot, j, to, there, counter[0])
        counter[0] += 1
        if to == "next_row":
            pl.when(has_next)(lambda: outgoing(*sent).start())
        else:
            outgoing(*sent).start()
        opened.append(sent)

    def finish(sent):
        if sent[2] == "next_row":
            pl.when(has_next)(lambda: outgoing(*sent).wait_send())
        else:
            outgoing(*sent).wait_send()

    for j in range(CHUNKS):
        for copy in staged[j]:
            copy.wait()
        send(0, j, "next_row", 4, open_common)
        after_common = counter[0]
        for r in range(COLUMNS):
            counter[0] = after_common

            @pl.when(x == r)
            def _(r=r, j=j):
                for to, there in first_sends(r, j):
                    send(0, j, to, there, open_role[r])

        counter[0] = after_common + 2
        send(0, j, "partner", 0, open_common)

    order = {}
    for r in range(COLUMNS):
        events = [
            (times[j], slot, j)
            for slot, times in EXPECTED[r].items()
            for j in range(CHUNKS)
            if times[j] is not None
        ]
        order[r] = sorted(events)

    def came_in(since, until):
        first = counter[0]
        most = first
        for r in range(COLUMNS):
            counter[0] = first

            @pl.when(x == r)
            def _(r=r):
                for time, slot, j in order[r]:
                    if not since <= time < until:
                        continue
                    there = part(slot, c, j)
                    remote(there, there, 0, rsem.at[slot, j], "partner").wait_recv()
                    for to, target in relays(r, slot, j):
                        send(slot, j, to, target, open_role[r])
                    if slot != 5:
                        send(slot, j, "partner", slot, open_role[r])

            most = max(most, counter[0])
        counter[0] = most

    def other_half(slot):
        for j in range(CHUNKS):
            there = part(slot, 1 - c, j)
            remote(there, there, 0, fsem.at[slot, j], "partner").wait_recv()

    def unpack(slot):
        for half in range(2):
            scf[slot, pl.ds(kv_heads * half, kv_heads), :] = kvb[slot, half, 0].astype(jnp.float32)
            for j in range(CHUNKS):
                at = 1 + 2 * piece * j
                to = pl.ds((half_tokens * half + piece * j) * kv_heads, piece * kv_heads)
                for which in range(2):
                    tile = kvb[slot, half, pl.ds(at + which * piece, piece)].astype(jnp.float32)
                    kvf[slot, which, to, :] = tile.reshape(piece * kv_heads, width)

    heads_per_core = kv_heads // 2
    factor = math.log2(math.e) / math.sqrt(width)

    def attend(slots, before, low, high, last=False):
        first = before is None

        @pl.loop(low, high, step=HEADS_AT_ONCE)
        def _(h0):
            def scale(s, h, which):
                at = kv_heads * (h // heads_per_core) + lax.rem(h, heads_per_core)
                one = scf[s, pl.ds(at + which * heads_per_core, 1), :]
                return jnp.concatenate([one] * (rows // width), axis=1)

            def scored(i):
                h = h0 + i
                out = []
                for s in slots:
                    k = kvf[s, 0, pl.ds(h, block, stride=kv_heads), :].astype(jnp.bfloat16)
                    raw = jnp.dot(k, qs[h], preferred_element_type=jnp.float32)
                    out.append(raw * (scale(s, h, 0) * factor) + bias[s])
                return out

            def topped(i, scores):
                h = h0 + i
                high_score = scores[0]
                for more in scores[1:]:
                    high_score = jnp.maximum(high_score, more)
                new_top = jnp.max(high_score, axis=0, keepdims=True)
                sums = shrink = None
                if not first:
                    old = top[h]
                    new_top = jnp.maximum(new_top, old)
                    shrink = jnp.exp2(old - new_top)
                    sums = total[h] * shrink
                if not last:
                    top[h] = new_top
                expos = []
                for score in scores:
                    expo = jnp.exp2(score - new_top)
                    added = jnp.sum(expo, axis=0, keepdims=True)
                    sums = added if sums is None else sums + added
                    expos.append(expo.astype(jnp.bfloat16))
                return sums, shrink, expos

            def added_up(i, found):
                h = h0 + i
                sums, shrink, expos = found
                summed = None if first else acc[h]
                unit = None if first else scale(before, h, 1)
                for s, expo in zip(slots, expos):
                    v = kvf[s, 1, pl.ds(h, block, stride=kv_heads), :].T.astype(jnp.bfloat16)
                    added = jnp.dot(v, expo, preferred_element_type=jnp.float32)
                    new_unit = scale(s, h, 1)
                    if summed is None:
                        summed = added
                    else:
                        ratio = unit / new_unit
                        if shrink is not None:
                            ratio = ratio * shrink
                        summed = summed * ratio + added
                    unit, shrink = new_unit, None
                if last:
                    result = (summed * (unit / sums)).T
                    o_ref[:, h] = result.reshape(half_tokens, group, width).astype(o_ref.dtype)
                else:
                    total[h] = sums
                    acc[h] = summed

            scores, found = {}, {}
            for n in range(HEADS_AT_ONCE + 2):
                if n < HEADS_AT_ONCE:
                    scores[n] = scored(n)
                if 0 <= n - 1 < HEADS_AT_ONCE:
                    found[n - 1] = topped(n - 1, scores.pop(n - 1))
                if 0 <= n - 2:
                    added_up(n - 2, found.pop(n - 2))

    len_copy.wait()
    lengths = jnp.broadcast_to(len_ref[...].astype(jnp.float32), (8, len_ref.shape[1]))
    docs = len_ref.shape[1]
    upto = lax.broadcasted_iota(jnp.int32, (docs, docs), 1) <= lax.broadcasted_iota(
        jnp.int32, (docs, docs), 0
    )
    ends = lax.dot_general(
        upto.astype(jnp.float32), lengths, (((1,), (1,)), ((), ())),
        precision=lax.Precision.HIGHEST, preferred_element_type=jnp.float32,
    )[:, 0:1]
    here = ctx * block + c * half_tokens + lax.broadcasted_iota(jnp.int32, (1, rows), 1) // group
    position = here.astype(jnp.float32)
    start = jnp.max(jnp.where(ends <= position, ends, 0.0), axis=0, keepdims=True)
    for s in range(5):
        key_position = (
            ctx * block - s * block + lax.broadcasted_iota(jnp.int32, (block, rows), 0)
        ).astype(jnp.float32)
        allowed = (key_position >= start) & (key_position <= position)
        bias[s] = jnp.where(allowed, 0.0, MASKED)

    q_copy.wait()

    @pl.loop(0, kv_heads)
    def _(h):
        qs[h] = qb[:, h].astype(jnp.float32).reshape(rows, width).T.astype(jnp.bfloat16)

    middle = kv_heads // 2
    other_half(0)
    unpack(0)
    attend([0], None, 0, middle)
    came_in(0.0, 3.5)
    attend([0], None, middle, kv_heads)
    came_in(3.5, 7.3)
    other_half(4)
    unpack(4)
    attend([4], 0, 0, 2)
    came_in(7.3, 7.5)
    attend([4], 0, 2, 6)
    came_in(7.5, 8.7)
    attend([4], 0, 6, kv_heads)
    came_in(8.7, 10.3)
    other_half(1)
    unpack(1)
    attend([1], 4, 0, middle)
    came_in(10.3, 10.5)
    attend([1], 4, middle, kv_heads)
    other_half(3)
    unpack(3)
    attend([3], 1, 0, middle)
    came_in(10.5, 12.0)
    attend([3], 1, middle, kv_heads)
    came_in(12.0, 99.0)
    other_half(2)
    unpack(2)
    attend([2], 3, 0, kv_heads, last=True)

    for sent in open_common:
        finish(sent)
    for r in range(COLUMNS):

        @pl.when(x == r)
        def _(r=r):
            for sent in open_role[r]:
                finish(sent)


def shards(
    queries, rotated_key_rows, unscaled_value_rows, key_block_scales, value_block_scales, doc_lengths
):
    tokens, heads, width = queries.shape
    kv_heads = rotated_key_rows.shape[1]
    group = heads // kv_heads
    rows = tokens * group
    scales = jnp.concatenate([key_block_scales, value_block_scales], axis=1)
    scales = jnp.broadcast_to(scales[:, :, None], (1, kv_heads, width))
    in_place = pl.BlockSpec(memory_space=pltpu.HBM)
    vmem = pl.BlockSpec(memory_space=pltpu.VMEM)
    out = pl.pallas_call(
        kernel,
        out_shape=jax.ShapeDtypeStruct((tokens, kv_heads, group, width), jnp.bfloat16),
        in_specs=[in_place] * 5,
        out_specs=vmem,
        scratch_shapes=[
            pltpu.VMEM((1, doc_lengths.shape[0]), jnp.int32),
            pltpu.VMEM((6, 2, 2 * tokens + 1, kv_heads, width), jnp.bfloat16),
            pltpu.VMEM((tokens, kv_heads, group, width), jnp.bfloat16),
            pltpu.VMEM((kv_heads, width, rows), jnp.bfloat16),
            pltpu.VMEM((5, 2, 2 * tokens * kv_heads, width), jnp.float32),
            pltpu.VMEM((5, 2 * kv_heads, width), jnp.float32),
            pltpu.VMEM((5, 2 * tokens, rows), jnp.float32),
            pltpu.VMEM((kv_heads, 1, rows), jnp.float32),
            pltpu.VMEM((kv_heads, 1, rows), jnp.float32),
            pltpu.VMEM((kv_heads, width, rows), jnp.float32),
            pltpu.SemaphoreType.DMA((3 + 2 * CHUNKS,)),
            pltpu.SemaphoreType.DMA((100,)),
            pltpu.SemaphoreType.DMA((6, CHUNKS)),
            pltpu.SemaphoreType.DMA((5, CHUNKS)),
        ],
        compiler_params=pltpu.CompilerParams(
            collective_id=0, has_side_effects=True, vmem_limit_bytes=24 * 1024 * 1024
        ),
    )(
        pltpu.with_memory_space_constraint(queries.reshape(tokens, kv_heads, group, width), pltpu.HBM),
        pltpu.with_memory_space_constraint(rotated_key_rows, pltpu.HBM),
        pltpu.with_memory_space_constraint(unscaled_value_rows, pltpu.HBM),
        scales,
        pltpu.with_memory_space_constraint(doc_lengths.reshape(1, -1), pltpu.HBM),
    )
    return out.reshape(tokens, heads, width)


def solution(mesh):
    return jax.shard_map(
        shards,
        mesh=mesh,
        in_specs=(
            P(("ctx", "tp"), None, None),
            P(("ctx", "tp"), None, None),
            P(("ctx", "tp"), None, None),
            P("ctx", "tp"),
            P("ctx", "tp"),
            P(),
        ),
        out_specs=P(("ctx", "tp"), None, None),
        check_vma=False,
    )
```

```python
import math

import jax
import jax.numpy as jnp
from jax import lax
from jax.experimental import pallas as pl
from jax.experimental.pallas import tpu as pltpu
from jax.sharding import PartitionSpec as P

CHUNKS = 4
COLUMNS = 4
MASKED = -1e30
HEADS_AT_ONCE = 2


def relays(role, slot, chunk):
    early = chunk < CHUNKS // 2
    out = []
    if slot == 4:
        if role in (2, 3) or (role == 1 and early):
            out.append(("left", 3))
        if role == 3:
            out.append(("right", 1))
    if slot == 1:
        if early and role in (0, 1, 2):
            out.append(("right", 2))
        if role == 3 and not early:
            out.append(("next_row", 5))
    if slot == 3:
        if (role == 1 and early) or (role in (2, 3) and not early):
            out.append(("left", 2))
    if slot == 5:
        if role == 0:
            out.extend([("left", 2), ("next_row", 3)])
        if role == 3:
            out.append(("right", 2))
    return out


def first_sends(role, chunk):
    out = []
    if role == 0:
        out.append(("left", 3))
    if role == 1 and chunk >= CHUNKS // 2:
        out.append(("left", 5))
    if role in (0, 1, 2):
        out.append(("right", 1))
    return out


EARLY = [3.0, 4.4, 5.8, 7.2]
EXPECTED = {
    0: {4: EARLY, 5: [None, None, 3.0, 4.4], 3: [6.0, 7.4, 8.6, 10.0], 1: [6.0, 7.4, 8.8, 10.2],
        2: [9.0, 10.4, 11.8, 13.2]},
    1: {4: EARLY, 1: EARLY, 3: [6.0, 7.4, 8.8, 10.2], 2: [9.0, 10.4, 11.8, 13.2]},
    2: {4: EARLY, 1: EARLY, 3: [6.0, 7.4, 8.8, 10.2], 2: [8.6, 10.0, 11.6, 13.0]},
    3: {4: EARLY, 1: EARLY, 3: EARLY, 5: [None, None, 8.8, 10.2], 2: [8.6, 10.0, 8.6, 10.0]},
}


def kernel(
    q_hbm, k_hbm, v_hbm, sc_hbm, len_hbm, o_ref,
    len_ref, kvb, qb, qs, kvf, scf, bias, top, total, acc,
    lsem, ssem, rsem, fsem,
):
    ctx, c = lax.axis_index("ctx"), lax.axis_index("tp")
    count = lax.axis_size("ctx")
    x = lax.rem(ctx, COLUMNS)
    row = ctx - x
    half_tokens, kv_heads, group, width = qb.shape[0], qb.shape[1], qb.shape[2], qb.shape[3]
    block = 2 * half_tokens
    piece = half_tokens // CHUNKS
    rows = half_tokens * group
    where = {
        "partner": (ctx, 1 - c),
        "right": (row + lax.rem(x + 1, COLUMNS), c),
        "left": (row + lax.rem(x + COLUMNS - 1, COLUMNS), c),
        "next_row": (lax.rem(ctx + COLUMNS, count), c),
    }
    last_row = (lax.rem(ctx + count - COLUMNS, count), c)

    def part(slot, half, j):
        if j == 0:
            return kvb.at[slot, half, pl.ds(0, 2 * piece + 1)]
        return kvb.at[slot, half, pl.ds(1 + 2 * piece * j, 2 * piece)]

    staged = [[] for _ in range(CHUNKS)]
    staged[0].append(pltpu.make_async_copy(sc_hbm, kvb.at[0, c, pl.ds(0, 1)], lsem.at[0]))
    for j in range(CHUNKS):
        at = 1 + 2 * piece * j
        source = pl.ds(piece * j, piece)
        staged[j].append(
            pltpu.make_async_copy(k_hbm.at[source], kvb.at[0, c, pl.ds(at, piece)], lsem.at[1 + 2 * j])
        )
        staged[j].append(
            pltpu.make_async_copy(
                v_hbm.at[source], kvb.at[0, c, pl.ds(at + piece, piece)], lsem.at[2 + 2 * j]
            )
        )
    for copies in staged:
        for copy in copies:
            copy.start()
    q_copy = pltpu.make_async_copy(q_hbm, qb, lsem.at[1 + 2 * CHUNKS])
    q_copy.start()
    len_copy = pltpu.make_async_copy(len_hbm, len_ref, lsem.at[2 + 2 * CHUNKS])
    len_copy.start()

    barrier = pltpu.get_barrier_semaphore()
    has_next = ctx < count - COLUMNS
    has_last = ctx >= COLUMNS

    def greet(other):
        pl.semaphore_signal(barrier, inc=1, device_id=other, device_id_type=pl.DeviceIdType.MESH)

    for other in ("partner", "right", "left"):
        greet(where[other])
    pl.when(has_next)(lambda: greet(where["next_row"]))
    pl.when(has_last)(lambda: greet(last_row))

    def stand_in(slot):
        for j in range(CHUNKS):
            at = 1 + 2 * piece * j
            source = pl.ds(piece * j, piece)
            for half, sem in ((c, rsem.at[slot, j]), (1 - c, fsem.at[slot, j])):
                if j == 0:
                    pltpu.make_async_copy(sc_hbm, kvb.at[slot, half, pl.ds(0, 1)], sem).start()
                pltpu.make_async_copy(
                    k_hbm.at[source], kvb.at[slot, half, pl.ds(at, piece)], sem
                ).start()
                pltpu.make_async_copy(
                    v_hbm.at[source], kvb.at[slot, half, pl.ds(at + piece, piece)], sem
                ).start()

    for slot in range(1, 5):
        pl.when(ctx < slot)(lambda slot=slot: stand_in(slot))
    pl.semaphore_wait(barrier, 3 + has_next.astype(jnp.int32) + has_last.astype(jnp.int32))

    counter = [0]
    open_common = []
    open_role = {r: [] for r in range(COLUMNS)}
    open_late = {(r, top): [] for r in range(COLUMNS) for top in (False, True)}

    def remote(src, dst, send, recv, to):
        return pltpu.make_async_remote_copy(
            src_ref=src, dst_ref=dst, send_sem=ssem.at[send], recv_sem=recv,
            device_id=where[to], device_id_type=pl.DeviceIdType.MESH,
        )

    def outgoing(slot, j, to, there, number):
        recv = fsem.at[there, j] if to == "partner" else rsem.at[there, j]
        return remote(part(slot, c, j), part(there, c, j), number, recv, to)

    def send(slot, j, to, there, opened):
        sent = (slot, j, to, there, counter[0])
        counter[0] += 1
        if to == "next_row":
            pl.when(has_next)(lambda: outgoing(*sent).start())
        else:
            outgoing(*sent).start()
        opened.append(sent)

    def finish(sent):
        if sent[2] == "next_row":
            pl.when(has_next)(lambda: outgoing(*sent).wait_send())
        else:
            outgoing(*sent).wait_send()

    for j in range(CHUNKS):
        for copy in staged[j]:
            copy.wait()
        send(0, j, "next_row", 4, open_common)
        after_common = counter[0]
        for r in range(COLUMNS):
            counter[0] = after_common

            @pl.when(x == r)
            def _(r=r, j=j):
                for to, there in first_sends(r, j):
                    send(0, j, to, there, open_role[r])

        counter[0] = after_common + 2
        send(0, j, "partner", 0, open_common)

    order = {}
    for r in range(COLUMNS):
        events = [
            (times[j], slot, j)
            for slot, times in EXPECTED[r].items()
            for j in range(CHUNKS)
            if times[j] is not None
        ]
        order[r] = sorted(events)

    def reach(r, to):
        return (r + (1 if to == "right" else COLUMNS - 1)) % COLUMNS

    def came_in(since, until):
        first = counter[0]
        most = first
        for r, top_row in open_late:
            counter[0] = first

            @pl.when((x == r) & (has_last != top_row))
            def _(r=r, top_row=top_row):
                opened = open_late[r, top_row]
                for time, slot, j in order[r]:
                    if not since <= time < until or (top_row and slot == 5 and r != 0):
                        continue
                    there = part(slot, c, j)
                    remote(there, there, 0, rsem.at[slot, j], "partner").wait_recv()
                    if top_row and r < slot < 5:
                        continue
                    for to, target in relays(r, slot, j):
                        if not (top_row and to != "next_row" and reach(r, to) < target < 5):
                            send(slot, j, to, target, opened)
                    if slot != 5:
                        send(slot, j, "partner", slot, opened)

            most = max(most, counter[0])
        counter[0] = most

    def other_half(slot):
        for j in range(CHUNKS):
            there = part(slot, 1 - c, j)
            remote(there, there, 0, fsem.at[slot, j], "partner").wait_recv()

    def unpack(slot):
        for half in range(2):
            scf[slot, pl.ds(kv_heads * half, kv_heads), :] = kvb[slot, half, 0].astype(jnp.float32)
            for j in range(CHUNKS):
                at = 1 + 2 * piece * j
                to = pl.ds((half_tokens * half + piece * j) * kv_heads, piece * kv_heads)
                for which in range(2):
                    tile = kvb[slot, half, pl.ds(at + which * piece, piece)].astype(jnp.float32)
                    kvf[slot, which, to, :] = tile.reshape(piece * kv_heads, width)

    heads_per_core = kv_heads // 2
    factor = math.log2(math.e) / math.sqrt(width)

    def attend(slots, before, low, high, last=False):
        first = before is None

        @pl.loop(low, high, step=HEADS_AT_ONCE)
        def _(h0):
            def scale(s, h, which):
                at = kv_heads * (h // heads_per_core) + lax.rem(h, heads_per_core)
                one = scf[s, pl.ds(at + which * heads_per_core, 1), :]
                return jnp.concatenate([one] * (rows // width), axis=1)

            def scored(i):
                h = h0 + i
                out = []
                for s in slots:
                    k = kvf[s, 0, pl.ds(h, block, stride=kv_heads), :].astype(jnp.bfloat16)
                    raw = jnp.dot(k, qs[h], preferred_element_type=jnp.float32)
                    out.append(raw * (scale(s, h, 0) * factor) + bias[s])
                return out

            def topped(i, scores):
                h = h0 + i
                high_score = scores[0]
                for more in scores[1:]:
                    high_score = jnp.maximum(high_score, more)
                new_top = jnp.max(high_score, axis=0, keepdims=True)
                sums = shrink = None
                if not first:
                    old = top[h]
                    new_top = jnp.maximum(new_top, old)
                    shrink = jnp.exp2(old - new_top)
                    sums = total[h] * shrink
                if not last:
                    top[h] = new_top
                expos = []
                for score in scores:
                    expo = jnp.exp2(score - new_top)
                    added = jnp.sum(expo, axis=0, keepdims=True)
                    sums = added if sums is None else sums + added
                    expos.append(expo.astype(jnp.bfloat16))
                return sums, shrink, expos

            def added_up(i, found):
                h = h0 + i
                sums, shrink, expos = found
                summed = None if first else acc[h]
                unit = None if first else scale(before, h, 1)
                for s, expo in zip(slots, expos):
                    v = kvf[s, 1, pl.ds(h, block, stride=kv_heads), :].T.astype(jnp.bfloat16)
                    added = jnp.dot(v, expo, preferred_element_type=jnp.float32)
                    new_unit = scale(s, h, 1)
                    if summed is None:
                        summed = added
                    else:
                        ratio = unit / new_unit
                        if shrink is not None:
                            ratio = ratio * shrink
                        summed = summed * ratio + added
                    unit, shrink = new_unit, None
                if last:
                    result = (summed * (unit / sums)).T
                    o_ref[:, h] = result.reshape(half_tokens, group, width).astype(o_ref.dtype)
                else:
                    total[h] = sums
                    acc[h] = summed

            scores, found = {}, {}
            for n in range(HEADS_AT_ONCE + 2):
                if n < HEADS_AT_ONCE:
                    scores[n] = scored(n)
                if 0 <= n - 1 < HEADS_AT_ONCE:
                    found[n - 1] = topped(n - 1, scores.pop(n - 1))
                if 0 <= n - 2:
                    added_up(n - 2, found.pop(n - 2))

    len_copy.wait()
    lengths = jnp.broadcast_to(len_ref[...].astype(jnp.float32), (8, len_ref.shape[1]))
    docs = len_ref.shape[1]
    upto = lax.broadcasted_iota(jnp.int32, (docs, docs), 1) <= lax.broadcasted_iota(
        jnp.int32, (docs, docs), 0
    )
    ends = lax.dot_general(
        upto.astype(jnp.float32), lengths, (((1,), (1,)), ((), ())),
        precision=lax.Precision.HIGHEST, preferred_element_type=jnp.float32,
    )[:, 0:1]
    here = ctx * block + c * half_tokens + lax.broadcasted_iota(jnp.int32, (1, rows), 1) // group
    position = here.astype(jnp.float32)
    start = jnp.max(jnp.where(ends <= position, ends, 0.0), axis=0, keepdims=True)
    for s in range(5):
        key_position = (
            ctx * block - s * block + lax.broadcasted_iota(jnp.int32, (block, rows), 0)
        ).astype(jnp.float32)
        allowed = (key_position >= start) & (key_position <= position)
        bias[s] = jnp.where(allowed, 0.0, MASKED)

    q_copy.wait()

    @pl.loop(0, kv_heads)
    def _(h):
        qs[h] = qb[:, h].astype(jnp.float32).reshape(rows, width).T.astype(jnp.bfloat16)

    middle = kv_heads // 2
    other_half(0)
    unpack(0)
    attend([0], None, 0, middle)
    came_in(0.0, 3.5)
    attend([0], None, middle, kv_heads)
    came_in(3.5, 7.3)
    other_half(4)
    unpack(4)
    attend([4], 0, 0, 2)
    came_in(7.3, 7.5)
    attend([4], 0, 2, 6)
    came_in(7.5, 8.7)
    attend([4], 0, 6, kv_heads)
    came_in(8.7, 10.3)
    other_half(1)
    unpack(1)
    attend([1], 4, 0, middle)
    came_in(10.3, 10.5)
    attend([1], 4, middle, kv_heads)
    other_half(3)
    unpack(3)
    attend([3], 1, 0, middle)
    came_in(10.5, 12.0)
    attend([3], 1, middle, kv_heads)
    came_in(12.0, 99.0)
    other_half(2)
    unpack(2)
    attend([2], 3, 0, kv_heads, last=True)

    for sent in open_common:
        finish(sent)
    for r in range(COLUMNS):

        @pl.when(x == r)
        def _(r=r):
            for sent in open_role[r]:
                finish(sent)

    for r, top_row in open_late:

        @pl.when((x == r) & (has_last != top_row))
        def _(r=r, top_row=top_row):
            for sent in open_late[r, top_row]:
                finish(sent)


def shards(
    queries, rotated_key_rows, unscaled_value_rows, key_block_scales, value_block_scales, doc_lengths
):
    tokens, heads, width = queries.shape
    kv_heads = rotated_key_rows.shape[1]
    group = heads // kv_heads
    rows = tokens * group
    scales = jnp.concatenate([key_block_scales, value_block_scales], axis=1)
    scales = jnp.broadcast_to(scales[:, :, None], (1, kv_heads, width))
    in_place = pl.BlockSpec(memory_space=pltpu.HBM)
    vmem = pl.BlockSpec(memory_space=pltpu.VMEM)
    out = pl.pallas_call(
        kernel,
        out_shape=jax.ShapeDtypeStruct((tokens, kv_heads, group, width), jnp.bfloat16),
        in_specs=[in_place] * 5,
        out_specs=vmem,
        scratch_shapes=[
            pltpu.VMEM((1, doc_lengths.shape[0]), jnp.int32),
            pltpu.VMEM((6, 2, 2 * tokens + 1, kv_heads, width), jnp.bfloat16),
            pltpu.VMEM((tokens, kv_heads, group, width), jnp.bfloat16),
            pltpu.VMEM((kv_heads, width, rows), jnp.bfloat16),
            pltpu.VMEM((5, 2, 2 * tokens * kv_heads, width), jnp.float32),
            pltpu.VMEM((5, 2 * kv_heads, width), jnp.float32),
            pltpu.VMEM((5, 2 * tokens, rows), jnp.float32),
            pltpu.VMEM((kv_heads, 1, rows), jnp.float32),
            pltpu.VMEM((kv_heads, 1, rows), jnp.float32),
            pltpu.VMEM((kv_heads, width, rows), jnp.float32),
            pltpu.SemaphoreType.DMA((3 + 2 * CHUNKS,)),
            pltpu.SemaphoreType.DMA((100,)),
            pltpu.SemaphoreType.DMA((6, CHUNKS)),
            pltpu.SemaphoreType.DMA((5, CHUNKS)),
        ],
        compiler_params=pltpu.CompilerParams(
            collective_id=0, has_side_effects=True, vmem_limit_bytes=24 * 1024 * 1024
        ),
    )(
        pltpu.with_memory_space_constraint(queries.reshape(tokens, kv_heads, group, width), pltpu.HBM),
        pltpu.with_memory_space_constraint(rotated_key_rows, pltpu.HBM),
        pltpu.with_memory_space_constraint(unscaled_value_rows, pltpu.HBM),
        scales,
        pltpu.with_memory_space_constraint(doc_lengths.reshape(1, -1), pltpu.HBM),
    )
    return out.reshape(tokens, heads, width)


def solution(mesh):
    return jax.shard_map(
        shards,
        mesh=mesh,
        in_specs=(
            P(("ctx", "tp"), None, None),
            P(("ctx", "tp"), None, None),
            P(("ctx", "tp"), None, None),
            P("ctx", "tp"),
            P("ctx", "tp"),
            P(),
        ),
        out_specs=P(("ctx", "tp"), None, None),
        check_vma=False,
    )
```

```python
import math

import jax
import jax.numpy as jnp
from jax import lax
from jax.experimental import pallas as pl
from jax.experimental.pallas import tpu as pltpu
from jax.sharding import PartitionSpec as P

CHUNKS = 8
COLUMNS = 4
MASKED = -1e30
HEADS_AT_ONCE = 2


def relays(role, slot, chunk):
    early = chunk < CHUNKS // 2
    out = []
    if slot == 4:
        if role in (2, 3) or (role == 1 and early):
            out.append(("left", 3))
        if role == 3:
            out.append(("right", 1))
    if slot == 1:
        if early and role in (0, 1, 2):
            out.append(("right", 2))
        if role == 3 and not early:
            out.append(("next_row", 5))
    if slot == 3:
        if (role == 1 and early) or (role in (2, 3) and not early):
            out.append(("left", 2))
    if slot == 5:
        if role == 0:
            out.extend([("left", 2), ("next_row", 3)])
        if role == 3:
            out.append(("right", 2))
    return out


def first_sends(role, chunk):
    out = []
    if role == 0:
        out.append(("left", 3))
    if role == 1 and chunk >= CHUNKS // 2:
        out.append(("left", 5))
    if role in (0, 1, 2):
        out.append(("right", 1))
    return out


EARLY = [3.0, 4.4, 5.8, 7.2]
EXPECTED = {
    0: {4: EARLY, 5: [None, None, 3.0, 4.4], 3: [6.0, 7.4, 8.6, 10.0], 1: [6.0, 7.4, 8.8, 10.2],
        2: [9.0, 10.4, 11.8, 13.2]},
    1: {4: EARLY, 1: EARLY, 3: [6.0, 7.4, 8.8, 10.2], 2: [9.0, 10.4, 11.8, 13.2]},
    2: {4: EARLY, 1: EARLY, 3: [6.0, 7.4, 8.8, 10.2], 2: [8.6, 10.0, 11.6, 13.0]},
    3: {4: EARLY, 1: EARLY, 3: EARLY, 5: [None, None, 8.8, 10.2], 2: [8.6, 10.0, 8.6, 10.0]},
}


def kernel(
    q_hbm, k_hbm, v_hbm, sc_hbm, len_hbm, o_ref,
    len_ref, kvb, qb, qs, kvf, scf, bias, top, total, acc,
    lsem, ssem, rsem, fsem,
):
    ctx, c = lax.axis_index("ctx"), lax.axis_index("tp")
    count = lax.axis_size("ctx")
    x = lax.rem(ctx, COLUMNS)
    row = ctx - x
    half_tokens, kv_heads, group, width = qb.shape[0], qb.shape[1], qb.shape[2], qb.shape[3]
    block = 2 * half_tokens
    piece = half_tokens // CHUNKS
    rows = half_tokens * group
    where = {
        "partner": (ctx, 1 - c),
        "right": (row + lax.rem(x + 1, COLUMNS), c),
        "left": (row + lax.rem(x + COLUMNS - 1, COLUMNS), c),
        "next_row": (lax.rem(ctx + COLUMNS, count), c),
    }
    last_row = (lax.rem(ctx + count - COLUMNS, count), c)

    def part(slot, half, j):
        if j == 0:
            return kvb.at[slot, half, pl.ds(0, 2 * piece + 1)]
        return kvb.at[slot, half, pl.ds(1 + 2 * piece * j, 2 * piece)]

    staged = [[] for _ in range(CHUNKS)]
    staged[0].append(pltpu.make_async_copy(sc_hbm, kvb.at[0, c, pl.ds(0, 1)], lsem.at[0]))
    for j in range(CHUNKS):
        at = 1 + 2 * piece * j
        source = pl.ds(piece * j, piece)
        staged[j].append(
            pltpu.make_async_copy(k_hbm.at[source], kvb.at[0, c, pl.ds(at, piece)], lsem.at[1 + 2 * j])
        )
        staged[j].append(
            pltpu.make_async_copy(
                v_hbm.at[source], kvb.at[0, c, pl.ds(at + piece, piece)], lsem.at[2 + 2 * j]
            )
        )
    for copies in staged:
        for copy in copies:
            copy.start()
    q_copy = pltpu.make_async_copy(q_hbm, qb, lsem.at[1 + 2 * CHUNKS])
    q_copy.start()
    len_copy = pltpu.make_async_copy(len_hbm, len_ref, lsem.at[2 + 2 * CHUNKS])
    len_copy.start()

    barrier = pltpu.get_barrier_semaphore()
    has_next = ctx < count - COLUMNS
    has_last = ctx >= COLUMNS

    def greet(other):
        pl.semaphore_signal(barrier, inc=1, device_id=other, device_id_type=pl.DeviceIdType.MESH)

    for other in ("partner", "right", "left"):
        greet(where[other])
    pl.when(has_next)(lambda: greet(where["next_row"]))
    pl.when(has_last)(lambda: greet(last_row))

    def stand_in(slot):
        for j in range(CHUNKS):
            at = 1 + 2 * piece * j
            source = pl.ds(piece * j, piece)
            for half, sem in ((c, rsem.at[slot, j]), (1 - c, fsem.at[slot, j])):
                if j == 0:
                    pltpu.make_async_copy(sc_hbm, kvb.at[slot, half, pl.ds(0, 1)], sem).start()
                pltpu.make_async_copy(
                    k_hbm.at[source], kvb.at[slot, half, pl.ds(at, piece)], sem
                ).start()
                pltpu.make_async_copy(
                    v_hbm.at[source], kvb.at[slot, half, pl.ds(at + piece, piece)], sem
                ).start()

    for slot in range(1, 5):
        pl.when(ctx < slot)(lambda slot=slot: stand_in(slot))
    pl.semaphore_wait(barrier, 3 + has_next.astype(jnp.int32) + has_last.astype(jnp.int32))

    counter = [0]
    open_common = []
    open_role = {r: [] for r in range(COLUMNS)}
    open_late = {(r, top): [] for r in range(COLUMNS) for top in (False, True)}

    def remote(src, dst, send, recv, to):
        return pltpu.make_async_remote_copy(
            src_ref=src, dst_ref=dst, send_sem=ssem.at[send], recv_sem=recv,
            device_id=where[to], device_id_type=pl.DeviceIdType.MESH,
        )

    def outgoing(slot, j, to, there, number):
        recv = fsem.at[there, j] if to == "partner" else rsem.at[there, j]
        return remote(part(slot, c, j), part(there, c, j), number, recv, to)

    def send(slot, j, to, there, opened):
        sent = (slot, j, to, there, counter[0])
        counter[0] += 1
        if to == "next_row":
            pl.when(has_next)(lambda: outgoing(*sent).start())
        else:
            outgoing(*sent).start()
        opened.append(sent)

    def finish(sent):
        if sent[2] == "next_row":
            pl.when(has_next)(lambda: outgoing(*sent).wait_send())
        else:
            outgoing(*sent).wait_send()

    for j in range(CHUNKS):
        for copy in staged[j]:
            copy.wait()
        send(0, j, "next_row", 4, open_common)
        after_common = counter[0]
        for r in range(COLUMNS):
            counter[0] = after_common

            @pl.when(x == r)
            def _(r=r, j=j):
                for to, there in first_sends(r, j):
                    send(0, j, to, there, open_role[r])

        counter[0] = after_common + 2
        send(0, j, "partner", 0, open_common)

    def due(times, j):
        time = times[j * len(times) // CHUNKS]
        return None if time is None else time - 0.7 * (1 - j % 2)

    order = {}
    for r in range(COLUMNS):
        events = [
            (due(times, j), slot, j)
            for slot, times in EXPECTED[r].items()
            for j in range(CHUNKS)
            if due(times, j) is not None
        ]
        order[r] = sorted(events)

    def reach(r, to):
        return (r + (1 if to == "right" else COLUMNS - 1)) % COLUMNS

    def came_in(since, until):
        first = counter[0]
        most = first
        for r, top_row in open_late:
            counter[0] = first

            @pl.when((x == r) & (has_last != top_row))
            def _(r=r, top_row=top_row):
                opened = open_late[r, top_row]
                for time, slot, j in order[r]:
                    if not since <= time < until or (top_row and slot == 5 and r != 0):
                        continue
                    there = part(slot, c, j)
                    remote(there, there, 0, rsem.at[slot, j], "partner").wait_recv()
                    if top_row and r < slot < 5:
                        continue
                    for to, target in relays(r, slot, j):
                        if not (top_row and to != "next_row" and reach(r, to) < target < 5):
                            send(slot, j, to, target, opened)
                    if slot != 5:
                        send(slot, j, "partner", slot, opened)

            most = max(most, counter[0])
        counter[0] = most

    def other_half(slot):
        for j in range(CHUNKS):
            there = part(slot, 1 - c, j)
            remote(there, there, 0, fsem.at[slot, j], "partner").wait_recv()

    def unpack(slot):
        for half in range(2):
            scf[slot, pl.ds(kv_heads * half, kv_heads), :] = kvb[slot, half, 0].astype(jnp.float32)
            for j in range(CHUNKS):
                at = 1 + 2 * piece * j
                to = pl.ds((half_tokens * half + piece * j) * kv_heads, piece * kv_heads)
                for which in range(2):
                    tile = kvb[slot, half, pl.ds(at + which * piece, piece)].astype(jnp.float32)
                    kvf[slot, which, to, :] = tile.reshape(piece * kv_heads, width)

    heads_per_core = kv_heads // 2
    factor = math.log2(math.e) / math.sqrt(width)

    def attend(slots, before, low, high, last=False):
        first = before is None

        @pl.loop(low, high, step=HEADS_AT_ONCE)
        def _(h0):
            def scale(s, h, which):
                at = kv_heads * (h // heads_per_core) + lax.rem(h, heads_per_core)
                one = scf[s, pl.ds(at + which * heads_per_core, 1), :]
                return jnp.concatenate([one] * (rows // width), axis=1)

            def scored(i):
                h = h0 + i
                out = []
                for s in slots:
                    k = kvf[s, 0, pl.ds(h, block, stride=kv_heads), :].astype(jnp.bfloat16)
                    raw = jnp.dot(k, qs[h], preferred_element_type=jnp.float32)
                    out.append(raw * (scale(s, h, 0) * factor) + bias[s])
                return out

            def topped(i, scores):
                h = h0 + i
                high_score = scores[0]
                for more in scores[1:]:
                    high_score = jnp.maximum(high_score, more)
                new_top = jnp.max(high_score, axis=0, keepdims=True)
                sums = shrink = None
                if not first:
                    old = top[h]
                    new_top = jnp.maximum(new_top, old)
                    shrink = jnp.exp2(old - new_top)
                    sums = total[h] * shrink
                if not last:
                    top[h] = new_top
                expos = []
                for score in scores:
                    expo = jnp.exp2(score - new_top)
                    added = jnp.sum(expo, axis=0, keepdims=True)
                    sums = added if sums is None else sums + added
                    expos.append(expo.astype(jnp.bfloat16))
                return sums, shrink, expos

            def added_up(i, found):
                h = h0 + i
                sums, shrink, expos = found
                summed = None if first else acc[h]
                unit = None if first else scale(before, h, 1)
                for s, expo in zip(slots, expos):
                    v = kvf[s, 1, pl.ds(h, block, stride=kv_heads), :].T.astype(jnp.bfloat16)
                    added = jnp.dot(v, expo, preferred_element_type=jnp.float32)
                    new_unit = scale(s, h, 1)
                    if summed is None:
                        summed = added
                    else:
                        ratio = unit / new_unit
                        if shrink is not None:
                            ratio = ratio * shrink
                        summed = summed * ratio + added
                    unit, shrink = new_unit, None
                if last:
                    result = (summed * (unit / sums)).T
                    o_ref[:, h] = result.reshape(half_tokens, group, width).astype(o_ref.dtype)
                else:
                    total[h] = sums
                    acc[h] = summed

            scores, found = {}, {}
            for n in range(HEADS_AT_ONCE + 2):
                if n < HEADS_AT_ONCE:
                    scores[n] = scored(n)
                if 0 <= n - 1 < HEADS_AT_ONCE:
                    found[n - 1] = topped(n - 1, scores.pop(n - 1))
                if 0 <= n - 2:
                    added_up(n - 2, found.pop(n - 2))

    len_copy.wait()
    lengths = jnp.broadcast_to(len_ref[...].astype(jnp.float32), (8, len_ref.shape[1]))
    docs = len_ref.shape[1]
    upto = lax.broadcasted_iota(jnp.int32, (docs, docs), 1) <= lax.broadcasted_iota(
        jnp.int32, (docs, docs), 0
    )
    ends = lax.dot_general(
        upto.astype(jnp.float32), lengths, (((1,), (1,)), ((), ())),
        precision=lax.Precision.HIGHEST, preferred_element_type=jnp.float32,
    )[:, 0:1]
    here = ctx * block + c * half_tokens + lax.broadcasted_iota(jnp.int32, (1, rows), 1) // group
    position = here.astype(jnp.float32)
    start = jnp.max(jnp.where(ends <= position, ends, 0.0), axis=0, keepdims=True)
    for s in range(5):
        key_position = (
            ctx * block - s * block + lax.broadcasted_iota(jnp.int32, (block, rows), 0)
        ).astype(jnp.float32)
        allowed = (key_position >= start) & (key_position <= position)
        bias[s] = jnp.where(allowed, 0.0, MASKED)

    q_copy.wait()

    @pl.loop(0, kv_heads)
    def _(h):
        qs[h] = qb[:, h].astype(jnp.float32).reshape(rows, width).T.astype(jnp.bfloat16)

    middle = kv_heads // 2
    other_half(0)
    unpack(0)
    attend([0], None, 0, middle)
    came_in(0.0, 3.5)
    attend([0], None, middle, kv_heads)
    came_in(3.5, 7.3)
    other_half(4)
    unpack(4)
    attend([4], 0, 0, 2)
    came_in(7.3, 7.5)
    attend([4], 0, 2, 6)
    came_in(7.5, 8.7)
    attend([4], 0, 6, kv_heads)
    came_in(8.7, 10.3)
    other_half(1)
    unpack(1)
    attend([1], 4, 0, middle)
    came_in(10.3, 10.5)
    attend([1], 4, middle, kv_heads)
    other_half(3)
    unpack(3)
    attend([3], 1, 0, middle)
    came_in(10.5, 12.0)
    attend([3], 1, middle, kv_heads)
    came_in(12.0, 99.0)
    other_half(2)
    unpack(2)
    attend([2], 3, 0, kv_heads, last=True)

    for sent in open_common:
        finish(sent)
    for r in range(COLUMNS):

        @pl.when(x == r)
        def _(r=r):
            for sent in open_role[r]:
                finish(sent)

    for r, top_row in open_late:

        @pl.when((x == r) & (has_last != top_row))
        def _(r=r, top_row=top_row):
            for sent in open_late[r, top_row]:
                finish(sent)


def shards(
    queries, rotated_key_rows, unscaled_value_rows, key_block_scales, value_block_scales, doc_lengths
):
    tokens, heads, width = queries.shape
    kv_heads = rotated_key_rows.shape[1]
    group = heads // kv_heads
    rows = tokens * group
    scales = jnp.concatenate([key_block_scales, value_block_scales], axis=1)
    scales = jnp.broadcast_to(scales[:, :, None], (1, kv_heads, width))
    in_place = pl.BlockSpec(memory_space=pltpu.HBM)
    vmem = pl.BlockSpec(memory_space=pltpu.VMEM)
    out = pl.pallas_call(
        kernel,
        out_shape=jax.ShapeDtypeStruct((tokens, kv_heads, group, width), jnp.bfloat16),
        in_specs=[in_place] * 5,
        out_specs=vmem,
        scratch_shapes=[
            pltpu.VMEM((1, doc_lengths.shape[0]), jnp.int32),
            pltpu.VMEM((6, 2, 2 * tokens + 1, kv_heads, width), jnp.bfloat16),
            pltpu.VMEM((tokens, kv_heads, group, width), jnp.bfloat16),
            pltpu.VMEM((kv_heads, width, rows), jnp.bfloat16),
            pltpu.VMEM((5, 2, 2 * tokens * kv_heads, width), jnp.float32),
            pltpu.VMEM((5, 2 * kv_heads, width), jnp.float32),
            pltpu.VMEM((5, 2 * tokens, rows), jnp.float32),
            pltpu.VMEM((kv_heads, 1, rows), jnp.float32),
            pltpu.VMEM((kv_heads, 1, rows), jnp.float32),
            pltpu.VMEM((kv_heads, width, rows), jnp.float32),
            pltpu.SemaphoreType.DMA((3 + 2 * CHUNKS,)),
            pltpu.SemaphoreType.DMA((200,)),
            pltpu.SemaphoreType.DMA((6, CHUNKS)),
            pltpu.SemaphoreType.DMA((5, CHUNKS)),
        ],
        compiler_params=pltpu.CompilerParams(
            collective_id=0, has_side_effects=True, vmem_limit_bytes=24 * 1024 * 1024
        ),
    )(
        pltpu.with_memory_space_constraint(queries.reshape(tokens, kv_heads, group, width), pltpu.HBM),
        pltpu.with_memory_space_constraint(rotated_key_rows, pltpu.HBM),
        pltpu.with_memory_space_constraint(unscaled_value_rows, pltpu.HBM),
        scales,
        pltpu.with_memory_space_constraint(doc_lengths.reshape(1, -1), pltpu.HBM),
    )
    return out.reshape(tokens, heads, width)


def solution(mesh):
    return jax.shard_map(
        shards,
        mesh=mesh,
        in_specs=(
            P(("ctx", "tp"), None, None),
            P(("ctx", "tp"), None, None),
            P(("ctx", "tp"), None, None),
            P("ctx", "tp"),
            P("ctx", "tp"),
            P(),
        ),
        out_specs=P(("ctx", "tp"), None, None),
        check_vma=False,
    )
```
